128 devices in a mesh: dp: 32 (over y, x, core), tensor: 4 (over z).
Axes of the slice: x: 4, y: 4, z: 4, core: 2. Of those that a mesh axis runs over, the one named last changes fastest.
Arguments:
- grad_query: bfloat16 [32, 8, 256, 2048], P('dp', None, None, 'tensor')
- grad_output: bfloat16 [32, 8, 256, 2048], P('dp', 'tensor')
- query_master: float32 [8, 256, 2048], P(None, 'dp', 'tensor'), may hold values from -4 to 4
- output_master: float32 [8, 256, 2048], P('tensor', 'dp'), may hold values from -4 to 4
- query_moment: float32 [8, 256, 2048], P(None, 'dp', 'tensor'), may hold values from 0.05 to 1
- output_moment: float32 [8, 256, 2048], P('tensor', 'dp'), may hold values from 0.05 to 1
- left_stat: float32 [4, 32, 3, 256, 256], P('tensor', 'dp')
- right_stat: float32 [4, 32, 3, 256, 256], P('tensor', 'dp')
- left_root: float32 [4, 32, 3, 256, 256], P('tensor', 'dp')
- right_root: float32 [4, 32, 3, 256, 256], P('tensor', 'dp')
- owner: int32 [4, 32], P('tensor'), may hold values from 0 to 31, as said below
Outputs:
- master_query: float32 [8, 256, 2048], P(None, 'dp', 'tensor')
- master_output: float32 [8, 256, 2048], P('tensor', 'dp')
- moment_query: float32 [8, 256, 2048], P(None, 'dp', 'tensor')
- moment_output: float32 [8, 256, 2048], P('tensor', 'dp')
- query_weight: bfloat16 [2048, 2048], P(None, 'tensor')
- output_weight: bfloat16 [2048, 2048], P('tensor')
- left_new: float32 [4, 32, 3, 256, 256], P('tensor', 'dp')
- right_new: float32 [4, 32, 3, 256, 256], P('tensor', 'dp')
The draws below stay inside these ranges and needn't reach their ends.
Inputs may be any that keep to these rules, and one draw needn't show every extreme that they name: `owner`: within one tensor group no device owns more than 3 blocks, and one device owns exactly 3.
All inputs are finite; a program needn't handle non-finite values.
Results may differ from the reference program's by a relative error of at most 0.0004.
Values may be sent and summed in bfloat16 or wider, within the bound.
A program may use at most 192 MiB of HBM per device.

```python
import math
import jax
import jax.numpy as jnp
from jax import lax

D = 2048
BLK = 256
HOLDERS = 32
GROUPS = 4
NB = 32
CAP = 3


def owner_line(seed_key):
    key_rich, key_rest, key_order = jax.random.split(seed_key, 3)
    richest = jax.random.randint(key_rich, (), 0, HOLDERS)
    others = jax.random.permutation(key_rest, (HOLDERS - 1) * CAP)[:NB - CAP] // CAP
    others = others + (others >= richest).astype(jnp.int32)
    joined = jnp.concatenate([jnp.full((CAP,), richest, dtype=jnp.int32), others.astype(jnp.int32)])
    return jax.random.permutation(key_order, joined)


def draw_owner(key, part):
    return jax.vmap(owner_line)(jax.random.split(jax.random.fold_in(key, 11), GROUPS))


def stat_shape():
    return (GROUPS, HOLDERS, CAP, BLK, BLK)


def symmetric(base, key_diag, diag_low, diag_high, noise):
    mirrored = (base + jnp.swapaxes(base, -1, -2)) * (noise * 0.70710678)
    diagonal = jnp.exp(jax.random.uniform(key_diag, base.shape[:-1], jnp.float32, math.log(diag_low), math.log(diag_high)))
    return mirrored + diagonal[..., None] * jnp.eye(BLK, dtype=jnp.float32)


def draw_left_stat(key, part):
    key_base, key_diag = jax.random.split(jax.random.fold_in(key, 21))
    return symmetric(jax.random.normal(key_base, stat_shape(), jnp.float32), key_diag, 1.0, 4.0, 0.1)


def draw_right_stat(key, part):
    key_base, key_diag = jax.random.split(jax.random.fold_in(key, 22))
    return symmetric(jax.random.normal(key_base, stat_shape(), jnp.float32), key_diag, 1.0, 4.0, 0.1)


def draw_left_root(key, part):
    key_base, key_diag = jax.random.split(jax.random.fold_in(key, 23))
    return symmetric(jax.random.normal(key_base, stat_shape(), jnp.float32), key_diag, 0.3, 1.0, 0.02)


def draw_right_root(key, part):
    key_base, key_diag = jax.random.split(jax.random.fold_in(key, 24))
    return symmetric(jax.random.normal(key_base, stat_shape(), jnp.float32), key_diag, 0.3, 1.0, 0.02)


def grad_scales(key_rows, key_cols, shape):
    rows_scale = jnp.exp(jax.random.uniform(key_rows, (1, shape[1], shape[2], 1), jnp.float32, math.log(0.3), math.log(3.0)))
    rising = jnp.exp(math.log(3.0) * jnp.arange(shape[2], dtype=jnp.float32) / shape[2])
    cols_scale = jnp.exp(jax.random.uniform(key_cols, (1, 1, 1, shape[3]), jnp.float32, math.log(0.3), math.log(3.0)))
    return 0.18 / math.sqrt(HOLDERS) * rows_scale * rising[None, None, :, None] * cols_scale


def draw_grad_query(key, part):
    shape = (HOLDERS, D // BLK, BLK, D)
    key_rows, key_cols, key_own = jax.random.split(jax.random.fold_in(key, 31), 3)
    scales = grad_scales(key_rows, key_cols, shape)
    return (jax.random.normal(key_own, shape, jnp.float32) * scales).astype(jnp.bfloat16)


def draw_grad_output(key, part):
    shape = (HOLDERS, D // BLK, BLK, D)
    key_rows, key_cols, key_own = jax.random.split(jax.random.fold_in(key, 41), 3)
    scales = grad_scales(key_rows, key_cols, shape)
    return (jax.random.normal(key_own, shape, jnp.float32) * scales).astype(jnp.bfloat16)


def level_of(stream_key, dims, pieces, low, high):
    def one(axis_at, blocks):
        draws = jax.random.uniform(jax.random.fold_in(jax.random.fold_in(stream_key, 6), axis_at), (blocks,), jnp.float32, low / len(pieces), high / len(pieces))
        return jnp.repeat(jnp.exp(draws), dims[axis_at] // blocks).reshape((-1,) + (1,) * (len(dims) - axis_at - 1))

    level = one(*pieces[0])
    for cut in pieces[1:]:
        level = level * one(*cut)
    return level


def scatter_about(own_key, shape, scale, reach, pieces=(), kind=jnp.bfloat16):
    loudness = level_of(own_key, shape, pieces, -0.22, 0.18) if pieces else 1.0
    values = jax.random.normal(own_key, shape, jnp.float32) * scale * loudness
    return jnp.minimum(jnp.maximum(values, -reach), reach).astype(kind)


def setup_inputs(seed: int = 0) -> dict:
    seeds = jax.random.split(jax.random.key(seed), 12)
    return {
        "grad_query": draw_grad_query(jax.random.fold_in(seeds[11], 71), 0),
        "grad_output": draw_grad_output(jax.random.fold_in(seeds[11], 71), 0),
        "query_master": scatter_about(seeds[2], (D // BLK, BLK, D), 0.5, 4.0, ((1, 32), (2, 4)), jnp.float32),
        "output_master": scatter_about(seeds[3], (D // BLK, BLK, D), 0.5, 4.0, ((0, 4), (1, 32)), jnp.float32),
        "query_moment": jnp.clip(jnp.exp(math.log(1.0) - 2.9957323 * jax.random.uniform(seeds[4], (D // BLK, BLK, D), jnp.float32) ** level_of(seeds[4], (D // BLK, BLK, D), ((1, 32), (2, 4)), -0.2, 0.2)), 0.05, 1.0),
        "output_moment": jnp.clip(jnp.exp(math.log(1.0) - 2.9957323 * jax.random.uniform(seeds[5], (D // BLK, BLK, D), jnp.float32) ** level_of(seeds[5], (D // BLK, BLK, D), ((0, 4), (1, 32)), -0.2, 0.2)), 0.05, 1.0),
        "left_stat": draw_left_stat(jax.random.fold_in(seeds[11], 71), 0),
        "right_stat": draw_right_stat(jax.random.fold_in(seeds[11], 71), 0),
        "left_root": draw_left_root(jax.random.fold_in(seeds[11], 71), 0),
        "right_root": draw_right_root(jax.random.fold_in(seeds[11], 71), 0),
        "owner": draw_owner(jax.random.fold_in(seeds[11], 71), 0),
    }


highest = lax.Precision.HIGHEST
stat_decay = 0.99
moment_decay = 0.9
learn_rate = 0.3
adam_eps = 1e-08
graft_eps = 1e-06

def refresh(blocks, left_stats, right_stats, left_inv, right_inv):
    outer_left = jnp.einsum('cij,ckj->cik', blocks, blocks, precision=highest)
    outer_right = jnp.einsum('cji,cjk->cik', blocks, blocks, precision=highest)
    left_fresh = stat_decay * left_stats + (1.0 - stat_decay) * outer_left
    right_fresh = stat_decay * right_stats + (1.0 - stat_decay) * outer_right
    scaled = jnp.einsum('cij,cjk->cik', left_inv, blocks, precision=highest)
    precond = jnp.einsum('cij,cjk->cik', scaled, right_inv, precision=highest)
    return (left_fresh, right_fresh, precond)

def to_blocks(matrix):
    stacks, height, extent = matrix.shape
    reshaped = matrix.reshape(stacks, height, extent // BLK, BLK).transpose(0, 2, 1, 3)
    return reshaped.reshape(stacks * (extent // BLK), height, BLK)

def from_blocks(blocks, stacks, extent):
    height = blocks.shape[1]
    reshaped = blocks.reshape(stacks, extent // BLK, height, BLK).transpose(0, 2, 1, 3)
    return reshaped.reshape(stacks, height, extent)

def slot_numbers(owner_row):
    total_rows = owner_row.shape[0]
    positions = jnp.arange(total_rows, dtype=jnp.int32)
    same_owner = owner_row[:, None] == owner_row[None, :]
    earlier = positions[None, :] < positions[:, None]
    return lax.optimization_barrier(jnp.sum((same_owner & earlier).astype(jnp.int32), axis=1)).astype(jnp.int32)

def reference(grad_query, grad_output, query_master, output_master, query_moment, output_moment, left_stat, right_stat, left_root, right_root, owner):
    slab_width = D // GROUPS
    row_blocks = D // BLK
    out_blocks = slab_width // BLK
    sum_query = lax.optimization_barrier(jnp.sum(grad_query.astype(jnp.float32), axis=0))
    sum_output = lax.optimization_barrier(jnp.sum(grad_output.astype(jnp.float32), axis=0))
    parts_query, parts_output, lefts, rights = ([], [], [], [])
    for group_id in range(GROUPS):
        blocks_query = to_blocks(sum_query[:, :, group_id * slab_width:(group_id + 1) * slab_width])
        blocks_output = to_blocks(sum_output[group_id * out_blocks:(group_id + 1) * out_blocks])
        blocks = jnp.concatenate([blocks_query, blocks_output], axis=0)
        owner_row = owner[group_id].astype(jnp.int32)
        slot_index = slot_numbers(owner_row)
        left_fresh, right_fresh, precond = refresh(blocks, left_stat[group_id][owner_row, slot_index], right_stat[group_id][owner_row, slot_index], left_root[group_id][owner_row, slot_index], right_root[group_id][owner_row, slot_index])
        lefts.append((stat_decay * left_stat[group_id]).at[owner_row, slot_index].set(left_fresh))
        rights.append((stat_decay * right_stat[group_id]).at[owner_row, slot_index].set(right_fresh))
        split_at = blocks_query.shape[0]
        parts_query.append(from_blocks(precond[:split_at], row_blocks, slab_width))
        parts_output.append(from_blocks(precond[split_at:], out_blocks, D))
    precond_query = jnp.concatenate(parts_query, axis=2)
    precond_output = jnp.concatenate(parts_output, axis=0)
    moment_query = moment_decay * query_moment + (1.0 - moment_decay) * sum_query * sum_query
    moment_output = moment_decay * output_moment + (1.0 - moment_decay) * sum_output * sum_output
    adam_query = sum_query / (jnp.sqrt(moment_query) + adam_eps)
    adam_output = sum_output / (jnp.sqrt(moment_output) + adam_eps)
    graft_query = jnp.sqrt(jnp.sum(adam_query * adam_query)) / (jnp.sqrt(jnp.sum(precond_query * precond_query)) + graft_eps)
    graft_output = jnp.sqrt(jnp.sum(adam_output * adam_output)) / (jnp.sqrt(jnp.sum(precond_output * precond_output)) + graft_eps)
    master_query = query_master - learn_rate * graft_query * precond_query
    master_output = output_master - learn_rate * graft_output * precond_output
    query_weight = master_query.reshape(D, D).astype(jnp.bfloat16)
    output_weight = master_output.reshape(D, D).astype(jnp.bfloat16)
    return (master_query, master_output, moment_query, moment_output, query_weight, output_weight, jnp.stack(lefts), jnp.stack(rights))
```

```python
import functools

import jax
import jax.numpy as jnp
from jax import lax
from jax.experimental import pallas as pl
from jax.experimental.pallas import tpu as pltpu
from jax.sharding import PartitionSpec as P

BLK = 256
N = 32
GROUPS = 4
CAP = 3
NB = 32
QB = 16
HEIGHT = BLK // N

highest = lax.Precision.HIGHEST
stat_decay = 0.99
moment_decay = 0.9
learn_rate = 0.3
adam_eps = 1e-08
graft_eps = 1e-06

MESH = pl.DeviceIdType.MESH


def tables(owner_row):
    ids = jnp.arange(NB, dtype=jnp.int32)
    same = owner_row[:, None] == owner_row[None, :]
    slot = jnp.sum((same & (ids[None, :] < ids[:, None])).astype(jnp.int32), axis=1)
    key = owner_row * CAP + slot
    places = jnp.arange(N * CAP, dtype=jnp.int32)
    source = NB + jnp.sum(jnp.where(key[None, :] == places[:, None], ids[None, :] - NB, 0), axis=1)
    return source, key


def kernel(
    source, key, gq, go, qmast, omast, qmom, omom, lstat, rstat, lroot, rroot,
    mq_out, mo_out, vq_out, vo_out, wq_out, wo_out, ln_out, rn_out,
    rq, ro, sq, so, blocks, gsend, gfull, pbuf, prec,
    qm, om, qv, ov, ls, rs, lr, rr, wq, wo,
    znorm, znet, nsend, nnet,
    in_sem, out_sem, rs_sq, rs_so, rs_rq, rs_ro, g_s, g_r, p_s, p_r, z_s, z_r, n_s, n_r, w_sq, w_so, w_rq, w_ro,
):
    me = lax.axis_index("dp")
    z = lax.axis_index("tensor")

    def peer(k):
        return lax.rem(me + k, N)

    loads = [
        pltpu.make_async_copy(src, dst, in_sem.at[i])
        for i, (src, dst) in enumerate(
            [(lroot, lr), (rroot, rr), (qmom, qv), (omom, ov), (qmast, qm), (omast, om), (lstat, ls), (rstat, rs)]
        )
    ]
    for copy in loads:
        copy.start()

    barrier = pltpu.get_barrier_semaphore()

    def greet(k, _):
        pl.semaphore_signal(barrier, inc=1, device_id={"dp": peer(k)}, device_id_type=MESH)
        return 0

    lax.fori_loop(1, N, greet, 0)
    for j in range(1, GROUPS):
        pl.semaphore_signal(
            barrier, inc=1, device_id={"tensor": lax.rem(z + j, GROUPS)}, device_id_type=MESH
        )
    pl.semaphore_wait(barrier, N - 1 + GROUPS - 1)

    def rows(d):
        return pl.ds(pl.multiple_of(d * HEIGHT, HEIGHT), HEIGHT)

    def grad_copies(to, slot):
        return (
            pltpu.make_async_remote_copy(
                gq.at[0, :, rows(to), :], rq.at[slot], rs_sq.at[to], rs_rq.at[slot],
                device_id={"dp": to}, device_id_type=MESH,
            ),
            pltpu.make_async_remote_copy(
                go.at[0, :, rows(to), :], ro.at[slot], rs_so.at[to], rs_ro.at[slot],
                device_id={"dp": to}, device_id_type=MESH,
            ),
        )

    def send_grads(k, _):
        for copy in grad_copies(peer(k), me):
            copy.start()
        return 0

    lax.fori_loop(1, N, send_grads, 0)
    own_q = pltpu.make_async_copy(gq.at[0, :, rows(me), :], rq.at[me], rs_rq.at[me])
    own_o = pltpu.make_async_copy(go.at[0, :, rows(me), :], ro.at[me], rs_ro.at[me])
    own_q.start()
    own_o.start()
    own_q.wait()
    own_o.wait()
    sq[...] = rq[me].astype(jnp.float32)
    so[...] = ro[me].astype(jnp.float32)

    def add_grads(k, _):
        frm = peer(k)
        for copy in grad_copies(frm, frm):
            copy.wait_recv()
        sq[...] += rq[frm].astype(jnp.float32)
        so[...] += ro[frm].astype(jnp.float32)
        return 0

    lax.fori_loop(1, N, add_grads, 0)

    for r in range(8):
        for c in range(2):
            blocks[r * 2 + c] = sq[r, :, c * BLK : (c + 1) * BLK]
    for r in range(2):
        for c in range(8):
            blocks[QB + r * 8 + c] = so[r, :, c * BLK : (c + 1) * BLK]
    blocks[NB] = jnp.zeros((HEIGHT, BLK), jnp.float32)

    def place(d, _):
        for s in range(CAP):
            gsend[d, s] = blocks[source[d * CAP + s]]
        return 0

    lax.fori_loop(0, N, place, 0)

    def g_copy(to, slot):
        return pltpu.make_async_remote_copy(
            gsend.at[to], gfull.at[:, rows(slot), :], g_s.at[to], g_r.at[slot],
            device_id={"dp": to}, device_id_type=MESH,
        )

    def send_blocks(k, _):
        g_copy(peer(k), me).start()
        return 0

    lax.fori_loop(1, N, send_blocks, 0)
    own_g = pltpu.make_async_copy(gsend.at[me], gfull.at[:, rows(me), :], g_r.at[me])
    own_g.start()

    loads[2].wait()
    loads[3].wait()
    fresh_q = moment_decay * qv[...] + (1.0 - moment_decay) * sq[...] * sq[...]
    qv[...] = fresh_q
    fresh_o = moment_decay * ov[...] + (1.0 - moment_decay) * so[...] * so[...]
    ov[...] = fresh_o
    adam_q = sq[...] / (jnp.sqrt(fresh_q) + adam_eps)
    adam_o = so[...] / (jnp.sqrt(fresh_o) + adam_eps)
    adam_q2 = jnp.sum(adam_q * adam_q)
    adam_o2 = jnp.sum(adam_o * adam_o)
    stores = [
        pltpu.make_async_copy(qv, vq_out, out_sem.at[0]),
        pltpu.make_async_copy(ov, vo_out, out_sem.at[1]),
    ]
    for copy in stores:
        copy.start()

    own_g.wait()

    def wait_blocks(k, _):
        frm = peer(k)
        g_copy(frm, frm).wait_recv()
        return 0

    lax.fori_loop(1, N, wait_blocks, 0)

    loads[0].wait()
    loads[1].wait()

    def dot(a, b, dims=((1,), (0,))):
        return lax.dot_general(a, b, (dims, ((), ())), precision=highest, preferred_element_type=jnp.float32)

    prec_q2 = 0.0
    prec_o2 = 0.0
    for s in range(CAP):
        pre = dot(dot(lr[s], gfull[s]), rr[s])
        pbuf[s] = pre
        square = jnp.sum(pre * pre)
        is_query = source[me * CAP + s] < QB
        prec_q2 = prec_q2 + jnp.where(is_query, square, 0.0)
        prec_o2 = prec_o2 + jnp.where(is_query, 0.0, square)

    def p_copy(to, slot):
        return pltpu.make_async_remote_copy(
            pbuf.at[:, rows(to), :], prec.at[pl.ds(slot * CAP, CAP)], p_s.at[to], p_r.at[slot],
            device_id={"dp": to}, device_id_type=MESH,
        )

    def send_prec(k, _):
        p_copy(peer(k), me).start()
        return 0

    lax.fori_loop(1, N, send_prec, 0)
    own_p = pltpu.make_async_copy(pbuf.at[:, rows(me), :], prec.at[pl.ds(me * CAP, CAP)], p_r.at[me])
    own_p.start()

    lane = lax.broadcasted_iota(jnp.int32, (8, 128), 1)
    mine = jnp.where(lane == 0, adam_q2, jnp.where(lane == 1, adam_o2, jnp.where(lane == 2, prec_q2, prec_o2)))
    znorm[...] = mine

    def z_copy(to, slot):
        return pltpu.make_async_remote_copy(
            znorm, znet.at[slot], z_s.at[to], z_r.at[slot], device_id={"tensor": to}, device_id_type=MESH
        )

    for j in range(1, GROUPS):
        z_copy(lax.rem(z + j, GROUPS), z).start()

    loads[6].wait()
    loads[7].wait()
    znet[z] = mine
    for j in range(1, GROUPS):
        frm = lax.rem(z + j, GROUPS)
        z_copy(frm, frm).wait_recv()
    total = znet[0] + znet[1] + znet[2] + znet[3]
    nsend[...] = total

    def n_copy(to, slot):
        return pltpu.make_async_remote_copy(
            nsend, nnet.at[slot], n_s.at[to], n_r.at[slot], device_id={"dp": to}, device_id_type=MESH
        )

    def send_norm(k, _):
        n_copy(peer(k), me).start()
        return 0

    lax.fori_loop(1, N, send_norm, 0)
    nnet[me] = total

    for s in range(CAP):
        g = gfull[s]
        ls[s] = stat_decay * ls[s] + (1.0 - stat_decay) * dot(g, g, ((1,), (1,)))
        rs[s] = stat_decay * rs[s] + (1.0 - stat_decay) * dot(g, g, ((0,), (0,)))
    stores += [
        pltpu.make_async_copy(ls, ln_out, out_sem.at[2]),
        pltpu.make_async_copy(rs, rn_out, out_sem.at[3]),
    ]
    stores[2].start()
    stores[3].start()

    own_p.wait()

    def wait_prec(k, _):
        frm = peer(k)
        p_copy(frm, frm).wait_recv()
        n_copy(frm, frm).wait_recv()
        return 0

    lax.fori_loop(1, N, wait_prec, 0)
    norms = jnp.sum(nnet[...], axis=0)

    def pick(i):
        return jnp.sum(jnp.where(lane == i, norms, 0.0), axis=1, keepdims=True)[0:1]

    scale_q = learn_rate * (jnp.sqrt(pick(0)) / (jnp.sqrt(pick(2)) + graft_eps))
    scale_o = learn_rate * (jnp.sqrt(pick(1)) / (jnp.sqrt(pick(3)) + graft_eps))

    loads[4].wait()
    loads[5].wait()
    for r in range(8):
        for c in range(2):
            cols = slice(c * BLK, (c + 1) * BLK)
            fresh = qm[r, :, cols] - scale_q * prec[key[r * 2 + c]]
            qm[r, :, cols] = fresh
            wq[r, :, cols] = fresh.astype(jnp.bfloat16)
    for r in range(2):
        for c in range(8):
            cols = slice(c * BLK, (c + 1) * BLK)
            fresh = om[r, :, cols] - scale_o * prec[key[QB + r * 8 + c]]
            om[r, :, cols] = fresh
            wo[r, :, cols] = fresh.astype(jnp.bfloat16)

    def w_copies(to, slot):
        return (
            pltpu.make_async_remote_copy(
                wq, wq_out.at[:, rows(slot), :], w_sq.at[to], w_rq.at[slot],
                device_id={"dp": to}, device_id_type=MESH,
            ),
            pltpu.make_async_remote_copy(
                wo, wo_out.at[:, rows(slot), :], w_so.at[to], w_ro.at[slot],
                device_id={"dp": to}, device_id_type=MESH,
            ),
        )

    def send_weights(k, _):
        for copy in w_copies(peer(k), me):
            copy.start()
        return 0

    lax.fori_loop(1, N, send_weights, 0)
    stores += [
        pltpu.make_async_copy(qm, mq_out, out_sem.at[4]),
        pltpu.make_async_copy(om, mo_out, out_sem.at[5]),
        pltpu.make_async_copy(wq, wq_out.at[:, rows(me), :], out_sem.at[6]),
        pltpu.make_async_copy(wo, wo_out.at[:, rows(me), :], out_sem.at[7]),
    ]
    for copy in stores[4:]:
        copy.start()

    def finish(k, _):
        d = peer(k)
        for copy in w_copies(d, d):
            copy.wait_recv()
            copy.wait_send()
        for copy in grad_copies(d, me):
            copy.wait_send()
        g_copy(d, me).wait_send()
        p_copy(d, me).wait_send()
        n_copy(d, me).wait_send()
        return 0

    lax.fori_loop(1, N, finish, 0)
    for j in range(1, GROUPS):
        z_copy(lax.rem(z + j, GROUPS), z).wait_send()
    for copy in stores:
        copy.wait()


def on_device(
    grad_query, grad_output, query_master, output_master, query_moment, output_moment,
    left_stat, right_stat, left_root, right_root, owner,
):
    source, key = tables(owner[0])
    f32, bf16 = jnp.float32, jnp.bfloat16
    stat = (CAP, BLK, BLK)
    qpiece, opiece = query_master.shape, output_master.shape
    anywhere = pl.BlockSpec(memory_space=pl.ANY)
    scalars = pl.BlockSpec(memory_space=pltpu.SMEM)
    dma = pltpu.SemaphoreType.DMA
    outs = pl.pallas_call(
        kernel,
        out_shape=[
            jax.ShapeDtypeStruct(qpiece, f32),
            jax.ShapeDtypeStruct(opiece, f32),
            jax.ShapeDtypeStruct(qpiece, f32),
            jax.ShapeDtypeStruct(opiece, f32),
            jax.ShapeDtypeStruct((8, BLK, 512), bf16),
            jax.ShapeDtypeStruct((2, BLK, 2048), bf16),
            jax.ShapeDtypeStruct(stat, f32),
            jax.ShapeDtypeStruct(stat, f32),
        ],
        in_specs=[scalars, scalars] + [anywhere] * 10,
        out_specs=[anywhere] * 8,
        scratch_shapes=[
            pltpu.VMEM((N,) + qpiece, bf16),
            pltpu.VMEM((N,) + opiece, bf16),
            pltpu.VMEM(qpiece, f32),
            pltpu.VMEM(opiece, f32),
            pltpu.VMEM((NB + 1, HEIGHT, BLK), f32),
            pltpu.VMEM((N, CAP, HEIGHT, BLK), f32),
            pltpu.VMEM(stat, f32),
            pltpu.VMEM(stat, f32),
            pltpu.VMEM((N * CAP, HEIGHT, BLK), f32),
            pltpu.VMEM(qpiece, f32),
            pltpu.VMEM(opiece, f32),
            pltpu.VMEM(qpiece, f32),
            pltpu.VMEM(opiece, f32),
            pltpu.VMEM(stat, f32),
            pltpu.VMEM(stat, f32),
            pltpu.VMEM(stat, f32),
            pltpu.VMEM(stat, f32),
            pltpu.VMEM(qpiece, bf16),
            pltpu.VMEM(opiece, bf16),
            pltpu.VMEM((8, 128), f32),
            pltpu.VMEM((GROUPS, 8, 128), f32),
            pltpu.VMEM((8, 128), f32),
            pltpu.VMEM((N, 8, 128), f32),
            dma((8,)),
            dma((8,)),
        ]
        + [dma((N,))] * 8
        + [dma((GROUPS,))] * 2
        + [dma((N,))] * 6,
        compiler_params=pltpu.CompilerParams(collective_id=0, has_side_effects=True, vmem_limit_bytes=60 << 20),
        name="shampoo",
    )(
        source, key, grad_query, grad_output, query_master, output_master, query_moment, output_moment,
        left_stat[0, 0], right_stat[0, 0], left_root[0, 0], right_root[0, 0],
    )
    mq, mo, vq, vo, wq, wo, ln, rn = outs
    return mq, mo, vq, vo, wq.reshape(-1, 512), wo.reshape(-1, 2048), ln[None, None], rn[None, None]


def solution(mesh):
    return jax.shard_map(
        on_device,
        mesh=mesh,
        in_specs=(
            P("dp", None, None, "tensor"),
            P("dp", "tensor", None, None),
            P(None, "dp", "tensor"),
            P("tensor", "dp", None),
            P(None, "dp", "tensor"),
            P("tensor", "dp", None),
            P("tensor", "dp", None, None, None),
            P("tensor", "dp", None, None, None),
            P("tensor", "dp", None, None, None),
            P("tensor", "dp", None, None, None),
            P("tensor", None),
        ),
        out_specs=(
            P(None, "dp", "tensor"),
            P("tensor", "dp", None),
            P(None, "dp", "tensor"),
            P("tensor", "dp", None),
            P(None, "tensor"),
            P("tensor", None),
            P("tensor", "dp", None, None, None),
            P("tensor", "dp", None, None, None),
        ),
        check_vma=False,
    )
```

```python
import functools

import jax
import jax.numpy as jnp
from jax import lax
from jax.experimental import pallas as pl
from jax.experimental.pallas import tpu as pltpu
from jax.sharding import PartitionSpec as P

BLK = 256
N = 32
GROUPS = 4
CAP = 3
NB = 32
QB = 16
HEIGHT = BLK // N
LIMIT = 36

highest = lax.Precision.HIGHEST
stat_decay = 0.99
moment_decay = 0.9
learn_rate = 0.3
adam_eps = 1e-08
graft_eps = 1e-06

MESH = pl.DeviceIdType.MESH


def tables(owner_row):
    ids = jnp.arange(NB, dtype=jnp.int32)
    same = owner_row[:, None] == owner_row[None, :]
    slot = jnp.sum((same & (ids[None, :] < ids[:, None])).astype(jnp.int32), axis=1)
    key = owner_row * CAP + slot
    places = jnp.arange(N * CAP, dtype=jnp.int32)
    source = NB + jnp.sum(jnp.where(key[None, :] == places[:, None], ids[None, :] - NB, 0), axis=1)
    return source, key


SIDE = 4


class Grads:
    def __init__(self, query, raw, refs, sems):
        self.query, self.raw = query, raw
        self.own, self.other, self.s1, self.rl1, self.rx1, self.t, self.rl2, self.rx2, self.total = refs
        self.sems = sems

    def at(self, ref, f, s=slice(None), r=slice(None)):
        return ref.at[r, s, f] if self.query else ref.at[r, f, s]


def halves(ref):
    rows = ref.shape[0]
    return pl.ds(0, rows // 2), pl.ds(rows // 2, rows // 2)


def kernel(
    source, key, gq, go, qmast, omast, qmom, omom, lstat, rstat, lroot, rroot,
    mq_out, mo_out, vq_out, vo_out, wq_out, wo_out, ln_out, rn_out,
    q_own, q_oth, q_s1, q_rl1, q_rx1, q_t, q_rl2, q_rx2, sq,
    o_own, o_oth, o_s1, o_rl1, o_rx1, o_t, o_rl2, o_rx2, so,
    blocks, gsend, gfull, pbuf, prec,
    qm, om, qv, ov, ls, rs, lr, rr, wq, wo,
    znorm, znet, nsend, nnet,
    in_sem, out_sem, own_sem, pair_s, pair_r, one_s, one_r, two_s, two_r,
    g_s, g_r, p_s, p_r, z_s, z_r, n_s, n_r, w_s, w_r, x_s, x_r,
):
    me = lax.axis_index("dp")
    z = lax.axis_index("tensor")
    core = lax.rem(me, 2)
    col = lax.rem(me // 2, SIDE)
    row = me // (2 * SIDE)
    other = 1 - core

    def peer(k):
        return lax.rem(me + k, N)

    def device(y, x, c):
        return {"dp": (y * SIDE + x) * 2 + c}

    def turn(i, k):
        return lax.rem(i + k + SIDE, SIDE)

    partner = device(row, col, other)
    east, west = device(row, turn(col, 1), core), device(row, turn(col, -1), core)
    south, north = device(turn(row, 1), col, core), device(turn(row, -1), col, core)

    def remote(src, dst, send, recv, to):
        return pltpu.make_async_remote_copy(src, dst, send, recv, device_id=to, device_id_type=MESH)

    Q = Grads(True, gq, (q_own, q_oth, q_s1, q_rl1, q_rx1, q_t, q_rl2, q_rx2, sq), 0)
    O = Grads(False, go, (o_own, o_oth, o_s1, o_rl1, o_rx1, o_t, o_rl2, o_rx2, so), 1)
    Q.f, Q.s, O.f, O.s = col, row, row, col
    Q.plus, Q.minus, Q.up, Q.down = east, west, south, north
    O.plus, O.minus, O.up, O.down = south, north, east, west
    both = (Q, O)
    order = (2, 1, 3, 0)

    def raw_chunk(a, k, c):
        f = turn(a.f, k)
        if a.query:
            return a.raw.at[0, :, :, f, c]
        return a.raw.at[0, :, f, :, c]

    own_loads = {}
    for k in order:
        for a in both:
            own_loads[a.sems, k] = pltpu.make_async_copy(
                raw_chunk(a, k, core), a.own.at[k], own_sem.at[a.sems, k]
            )
            own_loads[a.sems, k].start()
    loads = [
        pltpu.make_async_copy(src, dst, in_sem.at[i])
        for i, (src, dst) in enumerate(
            [(lroot, lr), (rroot, rr), (qmom, qv), (omom, ov), (qmast, qm), (omast, om), (lstat, ls), (rstat, rs)]
        )
    ]
    for copy in loads:
        copy.start()

    barrier = pltpu.get_barrier_semaphore()

    def greet(k, _):
        pl.semaphore_signal(barrier, inc=1, device_id={"dp": peer(k)}, device_id_type=MESH)
        return 0

    lax.fori_loop(1, N, greet, 0)
    for j in range(1, GROUPS):
        pl.semaphore_signal(
            barrier, inc=1, device_id={"tensor": lax.rem(z + j, GROUPS)}, device_id_type=MESH
        )
    pl.semaphore_wait(barrier, N - 1 + GROUPS - 1)

    sent = []

    def launch(copy):
        copy.start()
        sent.append(copy)
        return copy

    pairs = {}
    for k in order:
        for a in both:
            pairs[a.sems, k] = launch(
                remote(raw_chunk(a, k, other), a.other.at[k], pair_s.at[a.sems, k], pair_r.at[a.sems, k], partner)
            )

    def pair_sum(a, k):
        own_loads[a.sems, k].wait()
        pairs[a.sems, k].wait_recv()
        a.s1[k] = a.own[k].astype(jnp.float32) + a.other[k].astype(jnp.float32)

    def chunk_copies(a, send, recv, piece, rl, rx, plus, minus):
        lo, hi = halves(rx.at[0])
        return dict(
            relay_plus=remote(piece(2, lo), rl.at[0], send.at[0], recv.at[0], plus),
            relay_minus=remote(piece(2, hi), rl.at[1], send.at[1], recv.at[1], minus),
            near_plus=remote(piece(1, hi), rx.at[0, hi], send.at[2], recv.at[2], plus),
            near_minus=remote(piece(3, lo), rx.at[1, lo], send.at[3], recv.at[3], minus),
            last_plus=remote(piece(1, lo), rx.at[0, lo], send.at[4], recv.at[4], plus),
            last_minus=remote(piece(3, hi), rx.at[1, hi], send.at[5], recv.at[5], minus),
        )

    one, two = {}, {}
    for a in both:
        i = a.sems
        one[i] = chunk_copies(
            a, one_s.at[i], one_r.at[i], lambda k, r, a=a: a.s1.at[k, r], a.rl1, a.rx1, a.plus, a.minus
        )
        two[i] = chunk_copies(
            a, two_s.at[i], two_r.at[i], lambda k, r, a=a: a.t.at[turn(a.s, k), r], a.rl2, a.rx2, a.up, a.down
        )

    for a in both:
        pair_sum(a, 2)
        launch(one[a.sems]["relay_plus"])
        launch(one[a.sems]["relay_minus"])
    for a in both:
        pair_sum(a, 1)
        launch(one[a.sems]["near_plus"])
    for a in both:
        pair_sum(a, 3)
        launch(one[a.sems]["near_minus"])
    for a in both:
        pair_sum(a, 0)
    for a in both:
        lo, hi = halves(a.s1.at[0])
        one[a.sems]["relay_plus"].wait_recv()
        a.s1[1, lo] += a.rl1[0]
        launch(one[a.sems]["last_plus"])
        one[a.sems]["relay_minus"].wait_recv()
        a.s1[3, hi] += a.rl1[1]
        launch(one[a.sems]["last_minus"])
    for a in both:
        for name in ("near_plus", "near_minus", "last_plus", "last_minus"):
            one[a.sems][name].wait_recv()
        for k in (2, 1, 3, 0):
            s = turn(a.s, k)
            a.t[s] = a.s1[0, :, s] + a.rx1[0, :, s] + a.rx1[1, :, s]
            if k == 2:
                launch(two[a.sems]["relay_plus"])
                launch(two[a.sems]["relay_minus"])
            elif k == 1:
                launch(two[a.sems]["near_plus"])
            elif k == 3:
                launch(two[a.sems]["near_minus"])
    for a in both:
        lo, hi = halves(a.t.at[0])
        s = turn(a.s, 1)
        two[a.sems]["relay_plus"].wait_recv()
        a.t[s, lo] += a.rl2[0]
        launch(two[a.sems]["last_plus"])
        s = turn(a.s, 3)
        two[a.sems]["relay_minus"].wait_recv()
        a.t[s, hi] += a.rl2[1]
        launch(two[a.sems]["last_minus"])
    for a in both:
        for name in ("near_plus", "near_minus", "last_plus", "last_minus"):
            two[a.sems][name].wait_recv()
        a.total[...] = a.t[a.s] + a.rx2[0] + a.rx2[1]

    def rows(d):
        return pl.ds(pl.multiple_of(d * HEIGHT, HEIGHT), HEIGHT)

    for r in range(8):
        for c in range(2):
            blocks[r * 2 + c] = sq[r, :, c * BLK : (c + 1) * BLK]
    for r in range(2):
        for c in range(8):
            blocks[QB + r * 8 + c] = so[r, :, c * BLK : (c + 1) * BLK]
    blocks[NB] = jnp.zeros((HEIGHT, BLK), jnp.float32)

    def place(d, _):
        for s in range(CAP):
            gsend[d, s] = blocks[source[d * CAP + s]]
        return 0

    lax.fori_loop(0, N, place, 0)

    def g_copy(to, slot):
        return pltpu.make_async_remote_copy(
            gsend.at[to], gfull.at[:, rows(slot), :], g_s.at[to], g_r.at[slot],
            device_id={"dp": to}, device_id_type=MESH,
        )

    def send_blocks(k, _):
        g_copy(peer(k), me).start()
        return 0

    lax.fori_loop(1, N, send_blocks, 0)
    own_g = pltpu.make_async_copy(gsend.at[me], gfull.at[:, rows(me), :], g_r.at[me])
    own_g.start()

    loads[2].wait()
    loads[3].wait()
    fresh_q = moment_decay * qv[...] + (1.0 - moment_decay) * sq[...] * sq[...]
    qv[...] = fresh_q
    fresh_o = moment_decay * ov[...] + (1.0 - moment_decay) * so[...] * so[...]
    ov[...] = fresh_o
    adam_q = sq[...] / (jnp.sqrt(fresh_q) + adam_eps)
    adam_o = so[...] / (jnp.sqrt(fresh_o) + adam_eps)
    adam_q2 = jnp.sum(adam_q * adam_q)
    adam_o2 = jnp.sum(adam_o * adam_o)
    stores = [
        pltpu.make_async_copy(qv, vq_out, out_sem.at[0]),
        pltpu.make_async_copy(ov, vo_out, out_sem.at[1]),
    ]
    for copy in stores:
        copy.start()

    own_g.wait()

    def wait_blocks(k, _):
        frm = peer(k)
        g_copy(frm, frm).wait_recv()
        return 0

    lax.fori_loop(1, N, wait_blocks, 0)

    loads[0].wait()
    loads[1].wait()

    def dot(a, b, dims=((1,), (0,))):
        return lax.dot_general(a, b, (dims, ((), ())), precision=highest, preferred_element_type=jnp.float32)

    prec_q2 = 0.0
    prec_o2 = 0.0
    for s in range(CAP):
        pre = dot(dot(lr[s], gfull[s]), rr[s])
        pbuf[s] = pre
        square = jnp.sum(pre * pre)
        is_query = source[me * CAP + s] < QB
        prec_q2 = prec_q2 + jnp.where(is_query, square, 0.0)
        prec_o2 = prec_o2 + jnp.where(is_query, 0.0, square)

    def p_copy(to, slot):
        return pltpu.make_async_remote_copy(
            pbuf.at[:, rows(to), :], prec.at[pl.ds(slot * CAP, CAP)], p_s.at[to], p_r.at[slot],
            device_id={"dp": to}, device_id_type=MESH,
        )

    def send_prec(k, _):
        p_copy(peer(k), me).start()
        return 0

    lax.fori_loop(1, N, send_prec, 0)
    own_p = pltpu.make_async_copy(pbuf.at[:, rows(me), :], prec.at[pl.ds(me * CAP, CAP)], p_r.at[me])
    own_p.start()

    lane = lax.broadcasted_iota(jnp.int32, (8, 128), 1)
    mine = jnp.where(lane == 0, adam_q2, jnp.where(lane == 1, adam_o2, jnp.where(lane == 2, prec_q2, prec_o2)))
    znorm[...] = mine

    def z_copy(to, slot):
        return pltpu.make_async_remote_copy(
            znorm, znet.at[slot], z_s.at[to], z_r.at[slot], device_id={"tensor": to}, device_id_type=MESH
        )

    for j in range(1, GROUPS):
        z_copy(lax.rem(z + j, GROUPS), z).start()

    loads[6].wait()
    loads[7].wait()
    znet[z] = mine
    for j in range(1, GROUPS):
        frm = lax.rem(z + j, GROUPS)
        z_copy(frm, frm).wait_recv()
    total = znet[0] + znet[1] + znet[2] + znet[3]
    nsend[...] = total

    def n_copy(to, slot):
        return pltpu.make_async_remote_copy(
            nsend, nnet.at[slot], n_s.at[to], n_r.at[slot], device_id={"dp": to}, device_id_type=MESH
        )

    def send_norm(k, _):
        n_copy(peer(k), me).start()
        return 0

    lax.fori_loop(1, N, send_norm, 0)
    nnet[me] = total

    for s in range(CAP):
        g = gfull[s]
        ls[s] = stat_decay * ls[s] + (1.0 - stat_decay) * dot(g, g, ((1,), (1,)))
        rs[s] = stat_decay * rs[s] + (1.0 - stat_decay) * dot(g, g, ((0,), (0,)))
    stores += [
        pltpu.make_async_copy(ls, ln_out, out_sem.at[2]),
        pltpu.make_async_copy(rs, rn_out, out_sem.at[3]),
    ]
    stores[2].start()
    stores[3].start()

    own_p.wait()

    def wait_prec(k, _):
        frm = peer(k)
        p_copy(frm, frm).wait_recv()
        n_copy(frm, frm).wait_recv()
        return 0

    lax.fori_loop(1, N, wait_prec, 0)
    norms = jnp.sum(nnet[...], axis=0)

    def pick(i):
        return jnp.sum(jnp.where(lane == i, norms, 0.0), axis=1, keepdims=True)[0:1]

    scale_q = learn_rate * (jnp.sqrt(pick(0)) / (jnp.sqrt(pick(2)) + graft_eps))
    scale_o = learn_rate * (jnp.sqrt(pick(1)) / (jnp.sqrt(pick(3)) + graft_eps))

    loads[4].wait()
    loads[5].wait()
    for r in range(8):
        for c in range(2):
            cols = slice(c * BLK, (c + 1) * BLK)
            fresh = qm[r, :, cols] - scale_q * prec[key[r * 2 + c]]
            qm[r, :, cols] = fresh
            wq[r, :, cols] = fresh.astype(jnp.bfloat16)
    for r in range(2):
        for c in range(8):
            cols = slice(c * BLK, (c + 1) * BLK)
            fresh = om[r, :, cols] - scale_o * prec[key[QB + r * 8 + c]]
            om[r, :, cols] = fresh
            wo[r, :, cols] = fresh.astype(jnp.bfloat16)

    class Gather:
        pass

    GQ, GO = Gather(), Gather()
    for g, a, src, dst in ((GQ, Q, wq, wq_out), (GO, O, wo, wo_out)):
        g.a, g.src, g.dst, g.i = a, src, dst, a.sems

    def place_of(g, p, q, r=slice(None), c=None):
        f, s = turn(g.a.f, p), turn(g.a.s, q)
        y, x = (s, f) if g.a.query else (f, s)
        return g.dst.at[r, y * SIDE + x, core if c is None else c]

    def move(g, n, p, q, to, r=slice(None), fresh=False):
        src = g.src.at[r] if fresh else place_of(g, p, q, r)
        return remote(src, place_of(g, p, q, r), w_s.at[g.i, n], w_r.at[g.i, n], to)

    def incoming(g, n, p, q, r=slice(None)):
        there = place_of(g, p, q, r)
        remote(there, there, w_s.at[g.i, n], w_r.at[g.i, n], partner).wait_recv()

    def number(p, q):
        return (p % SIDE) * SIDE + q % SIDE

    def share(g, p, q, fresh=False):
        src = g.src if fresh else place_of(g, p, q)
        n = number(p, q)
        launch(remote(src, place_of(g, p, q), x_s.at[g.i, n], x_r.at[g.i, n], partner))

    gathers = (GQ, GO)

    def spread(g, p, fresh=False):
        base = 4 + 4 * (p % SIDE)
        launch(move(g, base + 0, p, 0, g.a.up, fresh=fresh))
        launch(move(g, base + 1, p, 0, g.a.down, fresh=fresh))

    def relay(g, p):
        base = 4 + 4 * (p % SIDE)
        lo, hi = halves(g.src)
        incoming(g, base + 0, p, -1)
        launch(move(g, base + 2, p, -1, g.a.up, lo))
        share(g, p, -1)
        incoming(g, base + 1, p, 1)
        launch(move(g, base + 3, p, 1, g.a.down, hi))
        share(g, p, 1)

    def far(g, p):
        base = 4 + 4 * (p % SIDE)
        lo, hi = halves(g.src)
        incoming(g, base + 2, p, 2, lo)
        incoming(g, base + 3, p, 2, hi)
        share(g, p, 2)

    for g in gathers:
        launch(move(g, 0, 0, 0, g.a.plus, fresh=True))
        launch(move(g, 1, 0, 0, g.a.minus, fresh=True))
    for g in gathers:
        spread(g, 0, fresh=True)
        share(g, 0, 0, fresh=True)
    stores += [
        pltpu.make_async_copy(qm, mq_out, out_sem.at[4]),
        pltpu.make_async_copy(om, mo_out, out_sem.at[5]),
        pltpu.make_async_copy(wq, place_of(GQ, 0, 0), out_sem.at[6]),
        pltpu.make_async_copy(wo, place_of(GO, 0, 0), out_sem.at[7]),
    ]
    for copy in stores[4:]:
        copy.start()
    for g in gathers:
        lo, hi = halves(g.src)
        incoming(g, 0, -1, 0)
        launch(move(g, 2, -1, 0, g.a.plus, lo))
        incoming(g, 1, 1, 0)
        launch(move(g, 3, 1, 0, g.a.minus, hi))
        spread(g, -1)
        spread(g, 1)
        share(g, -1, 0)
        share(g, 1, 0)
    for g in gathers:
        relay(g, 0)
    for g in gathers:
        lo, hi = halves(g.src)
        incoming(g, 2, 2, 0, lo)
        incoming(g, 3, 2, 0, hi)
        spread(g, 2)
        share(g, 2, 0)
    for p in (-1, 1, 2):
        for g in gathers:
            relay(g, p)
    for p in (0, -1, 1, 2):
        for g in gathers:
            far(g, p)
    for g in gathers:
        for p in range(SIDE):
            for q in range(SIDE):
                n = number(p, q)
                there = place_of(g, p, q, c=other)
                remote(there, there, x_s.at[g.i, n], x_r.at[g.i, n], partner).wait_recv()

    def finish(k, _):
        d = peer(k)
        g_copy(d, me).wait_send()
        p_copy(d, me).wait_send()
        n_copy(d, me).wait_send()
        return 0

    lax.fori_loop(1, N, finish, 0)
    for j in range(1, GROUPS):
        z_copy(lax.rem(z + j, GROUPS), z).wait_send()
    for copy in sent:
        copy.wait_send()
    for copy in stores:
        copy.wait()


def emit(*refs):
    count = (len(refs) - 1) // 2
    sem = refs[-1]
    copies = [pltpu.make_async_copy(refs[i], refs[count + i], sem.at[i]) for i in range(count)]
    for copy in copies:
        copy.start()
    for copy in copies:
        copy.wait()


def on_device(
    grad_query, grad_output, query_master, output_master, query_moment, output_moment,
    left_stat, right_stat, left_root, right_root, owner,
):
    source, key = tables(owner[0])
    f32, bf16 = jnp.float32, jnp.bfloat16
    stat = (CAP, BLK, BLK)
    qpiece, opiece = query_master.shape, output_master.shape
    anywhere = pl.BlockSpec(memory_space=pl.ANY)
    scalars = pl.BlockSpec(memory_space=pltpu.SMEM)
    dma = pltpu.SemaphoreType.DMA

    def sum_scratch(r, w):
        vm = pltpu.VMEM
        chunk, piece = (r, SIDE, HEIGHT, w), (r, HEIGHT, w)
        half = (r // 2, SIDE, HEIGHT, w), (r // 2, HEIGHT, w)
        return (
            vm((SIDE,) + chunk, bf16), vm((SIDE,) + chunk, bf16), vm((SIDE,) + chunk, f32),
            vm((2,) + half[0], f32), vm((2,) + chunk, f32), vm((SIDE,) + piece, f32),
            vm((2,) + half[1], f32), vm((2,) + piece, f32), vm(piece, f32),
        )

    outs = pl.pallas_call(
        kernel,
        out_shape=[
            jax.ShapeDtypeStruct(qpiece, f32),
            jax.ShapeDtypeStruct(opiece, f32),
            jax.ShapeDtypeStruct(qpiece, f32),
            jax.ShapeDtypeStruct(opiece, f32),
            jax.ShapeDtypeStruct((8, 16, 2, HEIGHT, 512), bf16),
            jax.ShapeDtypeStruct((2, 16, 2, HEIGHT, 2048), bf16),
            jax.ShapeDtypeStruct(stat, f32),
            jax.ShapeDtypeStruct(stat, f32),
        ],
        in_specs=[scalars, scalars] + [pl.BlockSpec(memory_space=pltpu.HBM)] * 10,
        out_specs=[anywhere] * 8,
        scratch_shapes=[
            *sum_scratch(8, 512),
            *sum_scratch(2, 2048),
            pltpu.VMEM((NB + 1, HEIGHT, BLK), f32),
            pltpu.VMEM((N, CAP, HEIGHT, BLK), f32),
            pltpu.VMEM(stat, f32),
            pltpu.VMEM(stat, f32),
            pltpu.VMEM((N * CAP, HEIGHT, BLK), f32),
            pltpu.VMEM(qpiece, f32),
            pltpu.VMEM(opiece, f32),
            pltpu.VMEM(qpiece, f32),
            pltpu.VMEM(opiece, f32),
            pltpu.VMEM(stat, f32),
            pltpu.VMEM(stat, f32),
            pltpu.VMEM(stat, f32),
            pltpu.VMEM(stat, f32),
            pltpu.VMEM(qpiece, bf16),
            pltpu.VMEM(opiece, bf16),
            pltpu.VMEM((8, 128), f32),
            pltpu.VMEM((GROUPS, 8, 128), f32),
            pltpu.VMEM((8, 128), f32),
            pltpu.VMEM((N, 8, 128), f32),
            dma((8,)),
            dma((8,)),
        ]
        + [dma((2, SIDE))] * 3
        + [dma((2, 6))] * 4
        + [dma((N,))] * 4
        + [dma((GROUPS,))] * 2
        + [dma((N,))] * 2
        + [dma((2, 20))] * 2
        + [dma((2, 16))] * 2,
        compiler_params=pltpu.CompilerParams(collective_id=0, has_side_effects=True, vmem_limit_bytes=LIMIT << 20),
        name="shampoo",
    )(
        source, key,
        *(
            pltpu.with_memory_space_constraint(x, pltpu.HBM)
            for x in (
                grad_query.reshape(1, 8, SIDE, SIDE, 2, HEIGHT, 512),
                grad_output.reshape(1, 2, SIDE, SIDE, 2, HEIGHT, 2048),
                query_master, output_master, query_moment, output_moment,
                left_stat[0, 0], right_stat[0, 0], left_root[0, 0], right_root[0, 0],
            )
        ),
    )
    mq, mo, vq, vo, wq, wo, ln, rn = pl.pallas_call(
        emit,
        out_shape=[jax.ShapeDtypeStruct(x.shape, x.dtype) for x in outs],
        in_specs=[anywhere] * 8,
        out_specs=[pl.BlockSpec(memory_space=pltpu.HBM)] * 8,
        scratch_shapes=[dma((8,))],
        compiler_params=pltpu.CompilerParams(vmem_limit_bytes=1 << 20),
        name="emit",
    )(*outs)
    return mq, mo, vq, vo, wq.reshape(-1, 512), wo.reshape(-1, 2048), ln[None, None], rn[None, None]


def solution(mesh):
    return jax.shard_map(
        on_device,
        mesh=mesh,
        in_specs=(
            P("dp", None, None, "tensor"),
            P("dp", "tensor", None, None),
            P(None, "dp", "tensor"),
            P("tensor", "dp", None),
            P(None, "dp", "tensor"),
            P("tensor", "dp", None),
            P("tensor", "dp", None, None, None),
            P("tensor", "dp", None, None, None),
            P("tensor", "dp", None, None, None),
            P("tensor", "dp", None, None, None),
            P("tensor", None),
        ),
        out_specs=(
            P(None, "dp", "tensor"),
            P("tensor", "dp", None),
            P(None, "dp", "tensor"),
            P("tensor", "dp", None),
            P(None, "tensor"),
            P("tensor", None),
            P("tensor", "dp", None, None, None),
            P("tensor", "dp", None, None, None),
        ),
        check_vma=False,
    )
```

```python
import functools

import jax
import jax.numpy as jnp
from jax import lax
from jax.experimental import pallas as pl
from jax.experimental.pallas import tpu as pltpu
from jax.sharding import PartitionSpec as P

BLK = 256
N = 32
GROUPS = 4
CAP = 3
NB = 32
QB = 16
HEIGHT = BLK // N
LIMIT = 36

highest = lax.Precision.HIGHEST
stat_decay = 0.99
moment_decay = 0.9
learn_rate = 0.3
adam_eps = 1e-08
graft_eps = 1e-06

MESH = pl.DeviceIdType.MESH


def tables(owner_row):
    ids = jnp.arange(NB, dtype=jnp.int32)
    same = owner_row[:, None] == owner_row[None, :]
    slot = jnp.sum((same & (ids[None, :] < ids[:, None])).astype(jnp.int32), axis=1)
    key = owner_row * CAP + slot
    places = jnp.arange(N * CAP, dtype=jnp.int32)
    source = NB + jnp.sum(jnp.where(key[None, :] == places[:, None], ids[None, :] - NB, 0), axis=1)
    return source, key


SIDE = 4


class Grads:
    def __init__(self, query, raw, refs, sems):
        self.query, self.raw = query, raw
        self.own, self.other, self.s1, self.rl1, self.rx1, self.t, self.rl2, self.rx2, self.total = refs
        self.sems = sems

    def at(self, ref, f, s=slice(None), r=slice(None)):
        return ref.at[r, s, f] if self.query else ref.at[r, f, s]


def halves(ref):
    rows = ref.shape[0]
    return pl.ds(0, rows // 2), pl.ds(rows // 2, rows // 2)


def kernel(
    source, key, gq, go, qmast, omast, qmom, omom, lstat, rstat, lroot, rroot,
    mq_out, mo_out, vq_out, vo_out, wq_out, wo_out, ln_out, rn_out,
    q_own, q_oth, q_s1, q_rl1, q_rx1, q_t, q_rl2, q_rx2, sq,
    o_own, o_oth, o_s1, o_rl1, o_rx1, o_t, o_rl2, o_rx2, so,
    blocks, gsend, gfull, pbuf, prec,
    qm, om, qv, ov, ls, rs, lr, rr, wq, wo,
    znorm, znet, nsend, nnet,
    in_sem, out_sem, own_sem, pair_s, pair_r, one_s, one_r, two_s, two_r,
    g_s, g_r, p_s, p_r, z_s, z_r, n_s, n_r, w_s, w_r, x_s, x_r,
):
    me = lax.axis_index("dp")
    z = lax.axis_index("tensor")
    core = lax.rem(me, 2)
    col = lax.rem(me // 2, SIDE)
    row = me // (2 * SIDE)
    other = 1 - core

    def everyone(act):
        def chip(j, _):
            y = lax.rem(row + 2 + 3 * (j // SIDE), SIDE)
            x = lax.rem(col + 2 + 3 * lax.rem(j, SIDE), SIDE)
            for c in range(2):
                act((y * SIDE + x) * 2 + lax.rem(core + c, 2))
            return 0

        lax.fori_loop(0, 10, chip, 0)
        lax.fori_loop(11, 16, chip, 0)
        act(row * 2 * SIDE + col * 2 + other)

    def device(y, x, c):
        return {"dp": (y * SIDE + x) * 2 + c}

    def turn(i, k):
        return lax.rem(i + k + SIDE, SIDE)

    partner = device(row, col, other)
    east, west = device(row, turn(col, 1), core), device(row, turn(col, -1), core)
    south, north = device(turn(row, 1), col, core), device(turn(row, -1), col, core)

    def remote(src, dst, send, recv, to):
        return pltpu.make_async_remote_copy(src, dst, send, recv, device_id=to, device_id_type=MESH)

    Q = Grads(True, gq, (q_own, q_oth, q_s1, q_rl1, q_rx1, q_t, q_rl2, q_rx2, sq), 0)
    O = Grads(False, go, (o_own, o_oth, o_s1, o_rl1, o_rx1, o_t, o_rl2, o_rx2, so), 1)
    Q.f, Q.s, O.f, O.s = col, row, row, col
    Q.plus, Q.minus, Q.up, Q.down = east, west, south, north
    O.plus, O.minus, O.up, O.down = south, north, east, west
    both = (Q, O)
    order = (2, 1, 3, 0)

    def raw_chunk(a, k, c):
        f = turn(a.f, k)
        if a.query:
            return a.raw.at[0, :, :, f, c]
        return a.raw.at[0, :, f, :, c]

    own_loads = {}
    for k in order:
        for a in both:
            own_loads[a.sems, k] = pltpu.make_async_copy(
                raw_chunk(a, k, core), a.own.at[k], own_sem.at[a.sems, k]
            )
            own_loads[a.sems, k].start()
    loads = [
        pltpu.make_async_copy(src, dst, in_sem.at[i])
        for i, (src, dst) in enumerate(
            [(lroot, lr), (rroot, rr), (qmom, qv), (omom, ov), (qmast, qm), (omast, om), (lstat, ls), (rstat, rs)]
        )
    ]
    for copy in loads:
        copy.start()

    barrier = pltpu.get_barrier_semaphore()

    for to in (partner, east, west, south, north):
        pl.semaphore_signal(barrier, inc=1, device_id=to, device_id_type=MESH)
    for j in range(1, GROUPS):
        pl.semaphore_signal(
            barrier, inc=1, device_id={"tensor": lax.rem(z + j, GROUPS)}, device_id_type=MESH
        )
    pl.semaphore_wait(barrier, 5 + GROUPS - 1)

    sent = []

    def launch(copy):
        copy.start()
        sent.append(copy)
        return copy

    def raw_slice(a, k, q, c):
        f, s = turn(a.f, k), turn(a.s, q)
        y, x = (s, f) if a.query else (f, s)
        return a.raw.at[0, :, y, x, c]

    pairs = {}
    for q in order:
        for k in order:
            for a in both:
                n = q * SIDE + k
                pairs[a.sems, q, k] = launch(
                    remote(
                        raw_slice(a, k, q, other), a.other.at[k, :, turn(a.s, q)],
                        pair_s.at[a.sems, n], pair_r.at[a.sems, n], partner,
                    )
                )

    def pair_sum(a, k, q):
        if q == order[0]:
            own_loads[a.sems, k].wait()
        pairs[a.sems, q, k].wait_recv()
        s = turn(a.s, q)
        a.s1[k, :, s] = a.own[k, :, s].astype(jnp.float32) + a.other[k, :, s].astype(jnp.float32)

    def chunk_copies(a, send, recv, piece, rl, rx, plus, minus):
        lo, hi = halves(a.total)
        return dict(
            relay_plus=remote(piece(2, lo), rl(0), send.at[0], recv.at[0], plus),
            relay_minus=remote(piece(2, hi), rl(1), send.at[1], recv.at[1], minus),
            near_plus=remote(piece(1, hi), rx(0, hi), send.at[2], recv.at[2], plus),
            near_minus=remote(piece(3, lo), rx(1, lo), send.at[3], recv.at[3], minus),
            last_plus=remote(piece(1, lo), rx(0, lo), send.at[4], recv.at[4], plus),
            last_minus=remote(piece(3, hi), rx(1, hi), send.at[5], recv.at[5], minus),
        )

    one, two = {}, {}
    for a in both:
        i = a.sems
        for q in order:
            s = turn(a.s, q)
            one[i, q] = chunk_copies(
                a, one_s.at[i, q], one_r.at[i, q],
                lambda k, r, a=a, s=s: a.s1.at[k, r, s],
                lambda w, a=a, s=s: a.rl1.at[w, :, s],
                lambda w, r, a=a, s=s: a.rx1.at[w, r, s],
                a.plus, a.minus,
            )
        two[i] = chunk_copies(
            a, two_s.at[i], two_r.at[i],
            lambda k, r, a=a: a.t.at[turn(a.s, k), r],
            lambda w, a=a: a.rl2.at[w],
            lambda w, r, a=a: a.rx2.at[w, r],
            a.up, a.down,
        )

    def open_slice(q):
        for a in both:
            pair_sum(a, 2, q)
            launch(one[a.sems, q]["relay_plus"])
            launch(one[a.sems, q]["relay_minus"])
        for a in both:
            pair_sum(a, 1, q)
            launch(one[a.sems, q]["near_plus"])
            pair_sum(a, 3, q)
            launch(one[a.sems, q]["near_minus"])

    def pass_slice(q):
        for a in both:
            lo, hi = halves(a.total)
            s = turn(a.s, q)
            one[a.sems, q]["relay_plus"].wait_recv()
            a.s1[1, lo, s] += a.rl1[0, :, s]
            launch(one[a.sems, q]["last_plus"])
            one[a.sems, q]["relay_minus"].wait_recv()
            a.s1[3, hi, s] += a.rl1[1, :, s]
            launch(one[a.sems, q]["last_minus"])
            pair_sum(a, 0, q)

    def close_slice(q):
        for a in both:
            s = turn(a.s, q)
            for name in ("near_plus", "near_minus", "last_plus", "last_minus"):
                one[a.sems, q][name].wait_recv()
            a.t[s] = a.s1[0, :, s] + a.rx1[0, :, s] + a.rx1[1, :, s]
            if q == 2:
                launch(two[a.sems]["relay_plus"])
                launch(two[a.sems]["relay_minus"])
            elif q == 1:
                launch(two[a.sems]["near_plus"])
            elif q == 3:
                launch(two[a.sems]["near_minus"])

    def pass_on(name, last, k, half):
        for a in both:
            s = turn(a.s, k)
            r = halves(a.total)[half]
            two[a.sems][name].wait_recv()
            a.t[s, r] += a.rl2[half]
            launch(two[a.sems][last])

    open_slice(2)
    open_slice(1)
    pass_slice(2)
    open_slice(3)
    pass_slice(1)
    close_slice(2)
    open_slice(0)
    pass_slice(3)
    close_slice(1)
    pass_on("relay_plus", "last_plus", 1, 0)
    pass_slice(0)
    close_slice(3)
    pass_on("relay_minus", "last_minus", 3, 1)
    close_slice(0)
    for a in both:
        for name in ("near_plus", "near_minus", "last_plus", "last_minus"):
            two[a.sems][name].wait_recv()
        a.total[...] = a.t[a.s] + a.rx2[0] + a.rx2[1]

    def rows(d):
        return pl.ds(pl.multiple_of(d * HEIGHT, HEIGHT), HEIGHT)

    for r in range(8):
        for c in range(2):
            blocks[r * 2 + c] = sq[r, :, c * BLK : (c + 1) * BLK]
    for r in range(2):
        for c in range(8):
            blocks[QB + r * 8 + c] = so[r, :, c * BLK : (c + 1) * BLK]
    blocks[NB] = jnp.zeros((HEIGHT, BLK), jnp.float32)

    def place(d):
        for s in range(CAP):
            gsend[d, s] = blocks[source[d * CAP + s]]

    def g_copy(to, slot):
        return pltpu.make_async_remote_copy(
            gsend.at[to], gfull.at[:, rows(slot), :], g_s.at[to], g_r.at[slot],
            device_id={"dp": to}, device_id_type=MESH,
        )

    def send_blocks(d):
        place(d)
        g_copy(d, me).start()

    everyone(send_blocks)
    place(me)
    own_g = pltpu.make_async_copy(gsend.at[me], gfull.at[:, rows(me), :], g_r.at[me])
    own_g.start()

    loads[2].wait()
    loads[3].wait()
    fresh_q = moment_decay * qv[...] + (1.0 - moment_decay) * sq[...] * sq[...]
    qv[...] = fresh_q
    fresh_o = moment_decay * ov[...] + (1.0 - moment_decay) * so[...] * so[...]
    ov[...] = fresh_o
    adam_q = sq[...] / (jnp.sqrt(fresh_q) + adam_eps)
    adam_o = so[...] / (jnp.sqrt(fresh_o) + adam_eps)
    adam_q2 = jnp.sum(jnp.sum(adam_q * adam_q, axis=0), axis=(0, 1), keepdims=True)
    adam_o2 = jnp.sum(jnp.sum(adam_o * adam_o, axis=0), axis=(0, 1), keepdims=True)
    stores = [
        pltpu.make_async_copy(qv, vq_out, out_sem.at[0]),
        pltpu.make_async_copy(ov, vo_out, out_sem.at[1]),
    ]
    for copy in stores:
        copy.start()

    own_g.wait()

    everyone(lambda d: g_copy(d, d).wait_recv())

    loads[0].wait()
    loads[1].wait()

    def dot(a, b, dims=((1,), (0,))):
        return lax.dot_general(a, b, (dims, ((), ())), precision=highest, preferred_element_type=jnp.float32)

    prec_q2 = jnp.zeros((1, BLK), jnp.float32)
    prec_o2 = jnp.zeros((1, BLK), jnp.float32)
    for s in range(CAP):
        pre = dot(dot(lr[s], gfull[s]), rr[s])
        pbuf[s] = pre
        square = jnp.sum(pre * pre, axis=0, keepdims=True)
        is_query = source[me * CAP + s] < QB
        prec_q2 = prec_q2 + jnp.where(is_query, square, 0.0)
        prec_o2 = prec_o2 + jnp.where(is_query, 0.0, square)
    prec_q2 = jnp.sum(prec_q2, axis=1, keepdims=True)
    prec_o2 = jnp.sum(prec_o2, axis=1, keepdims=True)

    def p_copy(to, slot):
        return pltpu.make_async_remote_copy(
            pbuf.at[:, rows(to), :], prec.at[pl.ds(slot * CAP, CAP)], p_s.at[to], p_r.at[slot],
            device_id={"dp": to}, device_id_type=MESH,
        )

    own_p = pltpu.make_async_copy(pbuf.at[:, rows(me), :], prec.at[pl.ds(me * CAP, CAP)], p_r.at[me])

    lane = lax.broadcasted_iota(jnp.int32, (1, 128), 1)
    mine = jnp.where(lane == 0, adam_q2, jnp.where(lane == 1, adam_o2, jnp.where(lane == 2, prec_q2, prec_o2)))
    znorm[...] = mine

    def z_copy(to, slot):
        return pltpu.make_async_remote_copy(
            znorm, znet.at[slot], z_s.at[to], z_r.at[slot], device_id={"tensor": to}, device_id_type=MESH
        )

    for j in range(1, GROUPS):
        z_copy(lax.rem(z + j, GROUPS), z).start()

    everyone(lambda d: p_copy(d, me).start())
    own_p.start()
    znet[z] = mine
    for j in range(1, GROUPS):
        frm = lax.rem(z + j, GROUPS)
        z_copy(frm, frm).wait_recv()
    total = znet[0] + znet[1] + znet[2] + znet[3]
    nsend[...] = total

    def n_copy(to, slot):
        return pltpu.make_async_remote_copy(
            nsend, nnet.at[slot], n_s.at[to], n_r.at[slot], device_id={"dp": to}, device_id_type=MESH
        )

    everyone(lambda d: n_copy(d, me).start())
    nnet[me] = total

    loads[6].wait()
    loads[7].wait()
    for s in range(CAP):
        g = gfull[s]
        ls[s] = stat_decay * ls[s] + (1.0 - stat_decay) * dot(g, g, ((1,), (1,)))
        rs[s] = stat_decay * rs[s] + (1.0 - stat_decay) * dot(g, g, ((0,), (0,)))
    stores += [
        pltpu.make_async_copy(ls, ln_out, out_sem.at[2]),
        pltpu.make_async_copy(rs, rn_out, out_sem.at[3]),
    ]
    stores[2].start()
    stores[3].start()

    own_p.wait()

    def wait_prec(d):
        p_copy(d, d).wait_recv()
        n_copy(d, d).wait_recv()

    everyone(wait_prec)
    norms = jnp.sum(nnet[...], axis=0)

    def pick(i):
        return jnp.sum(jnp.where(lane == i, norms, 0.0), axis=1, keepdims=True)

    scale_q = learn_rate * (jnp.sqrt(pick(0)) / (jnp.sqrt(pick(2)) + graft_eps))
    scale_o = learn_rate * (jnp.sqrt(pick(1)) / (jnp.sqrt(pick(3)) + graft_eps))

    loads[4].wait()
    loads[5].wait()
    class Gather:
        pass

    GQ, GO = Gather(), Gather()
    for g, a, src, dst in ((GQ, Q, wq, wq_out), (GO, O, wo, wo_out)):
        g.a, g.src, g.dst, g.i = a, src, dst, a.sems

    def place_of(g, p, q, r=slice(None), c=None):
        f, s = turn(g.a.f, p), turn(g.a.s, q)
        y, x = (s, f) if g.a.query else (f, s)
        return g.dst.at[r, y * SIDE + x, core if c is None else c]

    def move(g, n, p, q, to, r=slice(None), fresh=False):
        src = g.src.at[r] if fresh else place_of(g, p, q, r)
        return remote(src, place_of(g, p, q, r), w_s.at[g.i, n], w_r.at[g.i, n], to)

    def incoming(g, n, p, q, r=slice(None)):
        there = place_of(g, p, q, r)
        remote(there, there, w_s.at[g.i, n], w_r.at[g.i, n], partner).wait_recv()

    def number(p, q):
        return (p % SIDE) * SIDE + q % SIDE

    def share(g, p, q, fresh=False):
        src = g.src if fresh else place_of(g, p, q)
        n = number(p, q)
        launch(remote(src, place_of(g, p, q), x_s.at[g.i, n], x_r.at[g.i, n], partner))

    gathers = (GQ, GO)

    def spread(g, p, fresh=False):
        base = 4 + 4 * (p % SIDE)
        launch(move(g, base + 0, p, 0, g.a.up, fresh=fresh))
        launch(move(g, base + 1, p, 0, g.a.down, fresh=fresh))

    def relay(g, p):
        base = 4 + 4 * (p % SIDE)
        lo, hi = halves(g.src)
        incoming(g, base + 0, p, -1)
        launch(move(g, base + 2, p, -1, g.a.up, lo))
        share(g, p, -1)
        incoming(g, base + 1, p, 1)
        launch(move(g, base + 3, p, 1, g.a.down, hi))
        share(g, p, 1)

    def far(g, p):
        base = 4 + 4 * (p % SIDE)
        lo, hi = halves(g.src)
        incoming(g, base + 2, p, 2, lo)
        incoming(g, base + 3, p, 2, hi)
        share(g, p, 2)

    def masters_query():
        for r in range(8):
            for c in range(2):
                cols = slice(c * BLK, (c + 1) * BLK)
                fresh = qm[r, :, cols] - scale_q * prec[key[r * 2 + c]]
                qm[r, :, cols] = fresh
                wq[r, :, cols] = fresh.astype(jnp.bfloat16)

    def masters_output():
        for r in range(2):
            for c in range(8):
                cols = slice(c * BLK, (c + 1) * BLK)
                fresh = om[r, :, cols] - scale_o * prec[key[QB + r * 8 + c]]
                om[r, :, cols] = fresh
                wo[r, :, cols] = fresh.astype(jnp.bfloat16)

    for g, masters in ((GQ, masters_query), (GO, masters_output)):
        masters()
        launch(move(g, 0, 0, 0, g.a.plus, fresh=True))
        launch(move(g, 1, 0, 0, g.a.minus, fresh=True))
        spread(g, 0, fresh=True)
        share(g, 0, 0, fresh=True)
    stores += [
        pltpu.make_async_copy(qm, mq_out, out_sem.at[4]),
        pltpu.make_async_copy(om, mo_out, out_sem.at[5]),
        pltpu.make_async_copy(wq, place_of(GQ, 0, 0), out_sem.at[6]),
        pltpu.make_async_copy(wo, place_of(GO, 0, 0), out_sem.at[7]),
    ]
    for copy in stores[4:]:
        copy.start()
    for g in gathers:
        lo, hi = halves(g.src)
        incoming(g, 0, -1, 0)
        launch(move(g, 2, -1, 0, g.a.plus, lo))
        incoming(g, 1, 1, 0)
        launch(move(g, 3, 1, 0, g.a.minus, hi))
    for g in gathers:
        spread(g, -1)
        spread(g, 1)
        share(g, -1, 0)
        share(g, 1, 0)
    for g in gathers:
        relay(g, 0)
    for g in gathers:
        lo, hi = halves(g.src)
        incoming(g, 2, 2, 0, lo)
        incoming(g, 3, 2, 0, hi)
        spread(g, 2)
        share(g, 2, 0)
    for p in (-1, 1, 2):
        for g in gathers:
            relay(g, p)
    for p in (0, -1, 1, 2):
        for g in gathers:
            far(g, p)
    for g in gathers:
        for p in range(SIDE):
            for q in range(SIDE):
                n = number(p, q)
                there = place_of(g, p, q, c=other)
                remote(there, there, x_s.at[g.i, n], x_r.at[g.i, n], partner).wait_recv()

    def finish(d):
        g_copy(d, me).wait_send()
        p_copy(d, me).wait_send()
        n_copy(d, me).wait_send()

    everyone(finish)
    for j in range(1, GROUPS):
        z_copy(lax.rem(z + j, GROUPS), z).wait_send()
    for copy in sent:
        copy.wait_send()
    for copy in stores:
        copy.wait()


def emit(*refs):
    count = (len(refs) - 1) // 2
    sem = refs[-1]
    copies = [pltpu.make_async_copy(refs[i], refs[count + i], sem.at[i]) for i in range(count)]
    for copy in copies:
        copy.start()
    for copy in copies:
        copy.wait()


def on_device(
    grad_query, grad_output, query_master, output_master, query_moment, output_moment,
    left_stat, right_stat, left_root, right_root, owner,
):
    source, key = tables(owner[0])
    f32, bf16 = jnp.float32, jnp.bfloat16
    stat = (CAP, BLK, BLK)
    qpiece, opiece = query_master.shape, output_master.shape
    anywhere = pl.BlockSpec(memory_space=pl.ANY)
    scalars = pl.BlockSpec(memory_space=pltpu.SMEM)
    dma = pltpu.SemaphoreType.DMA

    def sum_scratch(r, w):
        vm = pltpu.VMEM
        chunk, piece = (r, SIDE, HEIGHT, w), (r, HEIGHT, w)
        half = (r // 2, SIDE, HEIGHT, w), (r // 2, HEIGHT, w)
        return (
            vm((SIDE,) + chunk, bf16), vm((SIDE,) + chunk, bf16), vm((SIDE,) + chunk, f32),
            vm((2,) + half[0], f32), vm((2,) + chunk, f32), vm((SIDE,) + piece, f32),
            vm((2,) + half[1], f32), vm((2,) + piece, f32), vm(piece, f32),
        )

    outs = pl.pallas_call(
        kernel,
        out_shape=[
            jax.ShapeDtypeStruct(qpiece, f32),
            jax.ShapeDtypeStruct(opiece, f32),
            jax.ShapeDtypeStruct(qpiece, f32),
            jax.ShapeDtypeStruct(opiece, f32),
            jax.ShapeDtypeStruct((8, 16, 2, HEIGHT, 512), bf16),
            jax.ShapeDtypeStruct((2, 16, 2, HEIGHT, 2048), bf16),
            jax.ShapeDtypeStruct(stat, f32),
            jax.ShapeDtypeStruct(stat, f32),
        ],
        in_specs=[scalars, scalars] + [pl.BlockSpec(memory_space=pltpu.HBM)] * 10,
        out_specs=[anywhere] * 8,
        scratch_shapes=[
            *sum_scratch(8, 512),
            *sum_scratch(2, 2048),
            pltpu.VMEM((NB + 1, HEIGHT, BLK), f32),
            pltpu.VMEM((N, CAP, HEIGHT, BLK), f32),
            pltpu.VMEM(stat, f32),
            pltpu.VMEM(stat, f32),
            pltpu.VMEM((N * CAP, HEIGHT, BLK), f32),
            pltpu.VMEM(qpiece, f32),
            pltpu.VMEM(opiece, f32),
            pltpu.VMEM(qpiece, f32),
            pltpu.VMEM(opiece, f32),
            pltpu.VMEM(stat, f32),
            pltpu.VMEM(stat, f32),
            pltpu.VMEM(stat, f32),
            pltpu.VMEM(stat, f32),
            pltpu.VMEM(qpiece, bf16),
            pltpu.VMEM(opiece, bf16),
            pltpu.VMEM((1, 128), f32),
            pltpu.VMEM((GROUPS, 1, 128), f32),
            pltpu.VMEM((1, 128), f32),
            pltpu.VMEM((N, 1, 128), f32),
            dma((8,)),
            dma((8,)),
        ]
        + [dma((2, SIDE)), dma((2, 16)), dma((2, 16))]
        + [dma((2, SIDE, 6))] * 2
        + [dma((2, 6))] * 2
        + [dma((N,))] * 4
        + [dma((GROUPS,))] * 2
        + [dma((N,))] * 2
        + [dma((2, 20))] * 2
        + [dma((2, 16))] * 2,
        compiler_params=pltpu.CompilerParams(collective_id=0, has_side_effects=True, vmem_limit_bytes=LIMIT << 20),
        name="shampoo",
    )(
        source, key,
        *(
            pltpu.with_memory_space_constraint(x, pltpu.HBM)
            for x in (
                grad_query.reshape(1, 8, SIDE, SIDE, 2, HEIGHT, 512),
                grad_output.reshape(1, 2, SIDE, SIDE, 2, HEIGHT, 2048),
                query_master, output_master, query_moment, output_moment,
                left_stat[0, 0], right_stat[0, 0], left_root[0, 0], right_root[0, 0],
            )
        ),
    )
    mq, mo, vq, vo, wq, wo, ln, rn = pl.pallas_call(
        emit,
        out_shape=[jax.ShapeDtypeStruct(x.shape, x.dtype) for x in outs],
        in_specs=[anywhere] * 8,
        out_specs=[pl.BlockSpec(memory_space=pltpu.HBM)] * 8,
        scratch_shapes=[dma((8,))],
        compiler_params=pltpu.CompilerParams(vmem_limit_bytes=1 << 20),
        name="emit",
    )(*outs)
    return mq, mo, vq, vo, wq.reshape(-1, 512), wo.reshape(-1, 2048), ln[None, None], rn[None, None]


def solution(mesh):
    return jax.shard_map(
        on_device,
        mesh=mesh,
        in_specs=(
            P("dp", None, None, "tensor"),
            P("dp", "tensor", None, None),
            P(None, "dp", "tensor"),
            P("tensor", "dp", None),
            P(None, "dp", "tensor"),
            P("tensor", "dp", None),
            P("tensor", "dp", None, None, None),
            P("tensor", "dp", None, None, None),
            P("tensor", "dp", None, None, None),
            P("tensor", "dp", None, None, None),
            P("tensor", None),
        ),
        out_specs=(
            P(None, "dp", "tensor"),
            P("tensor", "dp", None),
            P(None, "dp", "tensor"),
            P("tensor", "dp", None),
            P(None, "tensor"),
            P("tensor", None),
            P("tensor", "dp", None, None, None),
            P("tensor", "dp", None, None, None),
        ),
        check_vma=False,
    )
```

```python
import functools

import jax
import jax.numpy as jnp
from jax import lax
from jax.experimental import pallas as pl
from jax.experimental.pallas import tpu as pltpu
from jax.sharding import PartitionSpec as P

BLK = 256
N = 32
GROUPS = 4
CAP = 3
NB = 32
QB = 16
HEIGHT = BLK // N
LIMIT = 30

highest = lax.Precision.HIGHEST
stat_decay = 0.99
moment_decay = 0.9
learn_rate = 0.3
adam_eps = 1e-08
graft_eps = 1e-06

MESH = pl.DeviceIdType.MESH


SIDE = 4


class Grads:
    def __init__(self, query, raw, refs, sems):
        self.query, self.raw = query, raw
        self.own, self.other, self.s1, self.rl1, self.rx1, self.t, self.rl2, self.rx2, self.total = refs
        self.sems = sems


def halves(ref):
    rows = ref.shape[0]
    return pl.ds(0, rows // 2), pl.ds(rows // 2, rows // 2)


def kernel(
    owner, gq, go, qmast, omast, qmom, omom, lstat, rstat, lroot, rroot,
    mq_out, mo_out, vq_out, vo_out, wq_out, wo_out, ln_out, rn_out,
    q_own, q_oth, q_s1, q_rl1, q_rx1, q_t, q_rl2, q_rx2, sq,
    o_own, o_oth, o_s1, o_rl1, o_rx1, o_t, o_rl2, o_rx2, so,
    blocks, gsend, gfull, pbuf, prec,
    qm, om, qv, ov, ls, rs, lr, rr, wq, wo,
    znorm, znet, nsend, nnet, own_row, own_words, line, key, source,
    in_sem, out_sem, table_sem, own_sem, first_r, pair_s, pair_r, one_s, one_r, two_s, two_r,
    few_s, few_r, w_s, w_r, x_s, x_r,
):
    me = lax.axis_index("dp")
    z = lax.axis_index("tensor")
    core = lax.rem(me, 2)
    col = lax.rem(me // 2, SIDE)
    row = me // (2 * SIDE)
    other = 1 - core

    def everyone(act):
        def chip(j, _):
            y = lax.rem(row + 2 + 3 * (j // SIDE), SIDE)
            x = lax.rem(col + 2 + 3 * lax.rem(j, SIDE), SIDE)
            for c in range(2):
                act((y * SIDE + x) * 2 + lax.rem(core + c, 2))
            return 0

        lax.fori_loop(0, 10, chip, 0)
        lax.fori_loop(11, 16, chip, 0)
        act(row * 2 * SIDE + col * 2 + other)

    def device(y, x, c):
        return {"dp": (y * SIDE + x) * 2 + c}

    def turn(i, k):
        return lax.rem(i + k + SIDE, SIDE)

    partner = device(row, col, other)
    east, west = device(row, turn(col, 1), core), device(row, turn(col, -1), core)
    south, north = device(turn(row, 1), col, core), device(turn(row, -1), col, core)

    def remote(src, dst, send, recv, to):
        return pltpu.make_async_remote_copy(src, dst, send, recv, device_id=to, device_id_type=MESH)

    def arrived(ref, sem):
        remote(ref, ref, sem, sem, partner).wait_recv()

    def left(ref, sem):
        remote(ref, ref, sem, sem, partner).wait_send()

    read_row = pltpu.make_async_copy(owner, own_row, table_sem.at[0])
    read_words = pltpu.make_async_copy(owner, own_words, table_sem.at[1])
    read_row.start()
    read_words.start()
    Q = Grads(True, gq, (q_own, q_oth, q_s1, q_rl1, q_rx1, q_t, q_rl2, q_rx2, sq), 0)
    O = Grads(False, go, (o_own, o_oth, o_s1, o_rl1, o_rx1, o_t, o_rl2, o_rx2, so), 1)
    Q.f, Q.s, O.f, O.s = col, row, row, col
    Q.plus, Q.minus, Q.up, Q.down = east, west, south, north
    O.plus, O.minus, O.up, O.down = south, north, east, west
    both = (Q, O)
    order = (2, 1, 3, 0)

    own_loads = []
    for a in both:
        for f in range(SIDE):
            src = a.raw.at[0, :, :, f, core] if a.query else a.raw.at[0, :, f, :, core]
            own_loads.append(pltpu.make_async_copy(src, a.own.at[f], own_sem.at[a.sems, f]))
            own_loads[-1].start()
    loads = [
        pltpu.make_async_copy(src, dst, in_sem.at[i])
        for i, (src, dst) in enumerate(
            [(lroot, lr), (rroot, rr), (qmom, qv), (omom, ov), (qmast, qm), (omast, om), (lstat, ls), (rstat, rs)]
        )
    ]
    for copy in loads:
        copy.start()

    barrier = pltpu.get_barrier_semaphore()

    for to in (partner, east, west, south, north):
        pl.semaphore_signal(barrier, inc=1, device_id=to, device_id_type=MESH)
    for j in range(1, GROUPS):
        pl.semaphore_signal(
            barrier, inc=1, device_id={"tensor": lax.rem(z + j, GROUPS)}, device_id_type=MESH
        )

    lanes = lax.broadcasted_iota(jnp.int32, (1, 128), 1)
    read_row.wait()
    read_words.wait()
    row_of = own_row[...]
    spot = lanes[:, :NB]
    slot = jnp.zeros((1, NB), jnp.int32)
    for b in range(NB):
        slot = slot + jnp.where((row_of == own_words[0, b]) & (spot > b), 1, 0)
    line[0:1, 0:NB] = row_of * CAP + slot
    put_key = pltpu.make_async_copy(line.at[0:1], key, table_sem.at[2])
    put_key.start()
    put_key.wait()
    found = jnp.full((1, 128), NB, jnp.int32)
    for b in range(NB):
        found = jnp.where(lanes == key[0, b], b, found)
    line[1:2, :] = found
    put_source = pltpu.make_async_copy(line.at[1:2], source, table_sem.at[3])
    put_source.start()
    put_source.wait()
    pl.semaphore_wait(barrier, 5 + GROUPS - 1)

    def launch(copy):
        copy.start()
        return copy

    def raw_slice(a, k, q, c):
        f, s = turn(a.f, k), turn(a.s, q)
        y, x = (s, f) if a.query else (f, s)
        return a.raw.at[0, :, y, x, c]

    first = order[0]
    pairs = {}

    def pair_slice(q):
        for k in order:
            for a in both:
                recv = first_r.at[a.sems, k] if q == first else pair_r.at[a.sems, q]
                pairs[a.sems, q, k] = launch(
                    remote(
                        raw_slice(a, k, q, other), a.other.at[k, :, turn(a.s, q)], pair_s.at[a.sems], recv, partner
                    )
                )

    def pair_sum(a, k, q):
        s, f = turn(a.s, q), turn(a.f, k)
        if q == first:
            if k == first:
                for copy in own_loads[a.sems * SIDE : (a.sems + 1) * SIDE]:
                    copy.wait()
            pairs[a.sems, q, k].wait_recv()
        elif k == first:
            arrived(a.other.at[:, :, s], pair_r.at[a.sems, q])
        a.s1[k, :, s] = a.own[f, :, s].astype(jnp.float32) + a.other[k, :, s].astype(jnp.float32)

    def chunk_copies(a, send, recv, piece, rl, rx, plus, minus):
        lo, hi = halves(a.total)
        return dict(
            relay_plus=remote(piece(2, lo), rl(0), send, recv.at[0], plus),
            relay_minus=remote(piece(2, hi), rl(1), send, recv.at[0], minus),
            near_plus=remote(piece(1, hi), rx(0, hi), send, recv.at[1], plus),
            near_minus=remote(piece(3, lo), rx(1, lo), send, recv.at[1], minus),
            last_plus=remote(piece(1, lo), rx(0, lo), send, recv.at[1], plus),
            last_minus=remote(piece(3, hi), rx(1, hi), send, recv.at[1], minus),
        )

    one, two = {}, {}
    for a in both:
        i = a.sems
        for q in order:
            s = turn(a.s, q)
            one[i, q] = chunk_copies(
                a, one_s.at[i], one_r.at[i, q],
                lambda k, r, a=a, s=s: a.s1.at[k, r, s],
                lambda w, a=a, s=s: a.rl1.at[w, :, s],
                lambda w, r, a=a, s=s: a.rx1.at[w, r, s],
                a.plus, a.minus,
            )
        two[i] = chunk_copies(
            a, two_s.at[i], two_r.at[i],
            lambda k, r, a=a: a.t.at[turn(a.s, k), r],
            lambda w, a=a: a.rl2.at[w],
            lambda w, r, a=a: a.rx2.at[w, r],
            a.up, a.down,
        )

    def open_slice(q):
        for a in both:
            pair_sum(a, 2, q)
            launch(one[a.sems, q]["relay_plus"])
            launch(one[a.sems, q]["relay_minus"])
        for a in both:
            pair_sum(a, 1, q)
            launch(one[a.sems, q]["near_plus"])
            pair_sum(a, 3, q)
            launch(one[a.sems, q]["near_minus"])

    def pass_slice(q):
        for a in both:
            lo, hi = halves(a.total)
            s = turn(a.s, q)
            arrived(a.rl1.at[:, :, s], one_r.at[a.sems, q, 0])
            a.s1[1, lo, s] += a.rl1[0, :, s]
            launch(one[a.sems, q]["last_plus"])
            a.s1[3, hi, s] += a.rl1[1, :, s]
            launch(one[a.sems, q]["last_minus"])
            pair_sum(a, 0, q)

    def close_slice(q):
        for a in both:
            s = turn(a.s, q)
            arrived(a.rx1.at[:, :, s], one_r.at[a.sems, q, 1])
            a.t[s] = a.s1[0, :, s] + a.rx1[0, :, s] + a.rx1[1, :, s]
            if q == 2:
                launch(two[a.sems]["relay_plus"])
                launch(two[a.sems]["relay_minus"])
            elif q == 1:
                launch(two[a.sems]["near_plus"])
            elif q == 3:
                launch(two[a.sems]["near_minus"])

    def pass_on(last, k, half):
        for a in both:
            s = turn(a.s, k)
            r = halves(a.total)[half]
            if half == 0:
                arrived(a.rl2, two_r.at[a.sems, 0])
            a.t[s, r] += a.rl2[half]
            launch(two[a.sems][last])

    pair_slice(2)
    pair_slice(1)
    open_slice(2)
    pair_slice(3)
    open_slice(1)
    pair_slice(0)
    pass_slice(2)
    open_slice(3)
    pass_slice(1)
    close_slice(2)
    open_slice(0)
    pass_slice(3)
    close_slice(1)
    pass_on("last_plus", 1, 0)
    pass_slice(0)
    close_slice(3)
    pass_on("last_minus", 3, 1)
    close_slice(0)
    for a in both:
        arrived(a.rx2, two_r.at[a.sems, 1])
        a.total[...] = a.t[a.s] + a.rx2[0] + a.rx2[1]

    def rows(d):
        return pl.ds(pl.multiple_of(d * HEIGHT, HEIGHT), HEIGHT)

    for r in range(8):
        for c in range(2):
            blocks[r * 2 + c] = sq[r, :, c * BLK : (c + 1) * BLK]
    for r in range(2):
        for c in range(8):
            blocks[QB + r * 8 + c] = so[r, :, c * BLK : (c + 1) * BLK]
    blocks[NB] = jnp.zeros((HEIGHT, BLK), jnp.float32)

    def place(d):
        for s in range(CAP):
            gsend[d, s] = blocks[source[0, d * CAP + s]]

    def g_copy(to, slot):
        return pltpu.make_async_remote_copy(
            gsend.at[to], gfull.at[:, rows(slot), :], few_s.at[0], few_r.at[0],
            device_id={"dp": to}, device_id_type=MESH,
        )

    def send_blocks(d):
        place(d)
        g_copy(d, me).start()

    everyone(send_blocks)
    place(me)
    own_g = pltpu.make_async_copy(gsend.at[me], gfull.at[:, rows(me), :], few_r.at[0])
    own_g.start()

    loads[2].wait()
    loads[3].wait()
    fresh_q = moment_decay * qv[...] + (1.0 - moment_decay) * sq[...] * sq[...]
    qv[...] = fresh_q
    fresh_o = moment_decay * ov[...] + (1.0 - moment_decay) * so[...] * so[...]
    ov[...] = fresh_o
    adam_q = sq[...] / (jnp.sqrt(fresh_q) + adam_eps)
    adam_o = so[...] / (jnp.sqrt(fresh_o) + adam_eps)
    adam_q2 = jnp.sum(jnp.sum(adam_q * adam_q, axis=0), axis=(0, 1), keepdims=True)
    adam_o2 = jnp.sum(jnp.sum(adam_o * adam_o, axis=0), axis=(0, 1), keepdims=True)
    stores = [
        pltpu.make_async_copy(qv, vq_out, out_sem.at[0]),
        pltpu.make_async_copy(ov, vo_out, out_sem.at[1]),
    ]
    for copy in stores:
        copy.start()

    arrived(gfull, few_r.at[0])

    loads[0].wait()
    loads[1].wait()

    def dot(a, b, dims=((1,), (0,))):
        return lax.dot_general(a, b, (dims, ((), ())), precision=highest, preferred_element_type=jnp.float32)

    prec_q2 = jnp.zeros((1, BLK), jnp.float32)
    prec_o2 = jnp.zeros((1, BLK), jnp.float32)
    for s in range(CAP):
        pre = dot(dot(lr[s], gfull[s]), rr[s])
        pbuf[s] = pre
        square = jnp.sum(pre * pre, axis=0, keepdims=True)
        is_query = source[0, me * CAP + s] < QB
        prec_q2 = prec_q2 + jnp.where(is_query, square, 0.0)
        prec_o2 = prec_o2 + jnp.where(is_query, 0.0, square)
    prec_q2 = jnp.sum(prec_q2, axis=1, keepdims=True)
    prec_o2 = jnp.sum(prec_o2, axis=1, keepdims=True)

    def p_copy(to, slot):
        return pltpu.make_async_remote_copy(
            pbuf.at[:, rows(to), :], prec.at[pl.ds(slot * CAP, CAP)], few_s.at[1], few_r.at[1],
            device_id={"dp": to}, device_id_type=MESH,
        )

    own_p = pltpu.make_async_copy(pbuf.at[:, rows(me), :], prec.at[pl.ds(me * CAP, CAP)], few_r.at[1])

    lane = lax.broadcasted_iota(jnp.int32, (1, 128), 1)
    mine = jnp.where(lane == 0, adam_q2, jnp.where(lane == 1, adam_o2, jnp.where(lane == 2, prec_q2, prec_o2)))
    znorm[...] = mine

    def z_copy(to, slot):
        return pltpu.make_async_remote_copy(
            znorm, znet.at[slot], few_s.at[2], few_r.at[2], device_id={"tensor": to}, device_id_type=MESH
        )

    for j in range(1, GROUPS):
        z_copy(lax.rem(z + j, GROUPS), z).start()

    everyone(lambda d: p_copy(d, me).start())
    own_p.start()
    znet[z] = mine
    arrived(znet.at[pl.ds(0, GROUPS - 1)], few_r.at[2])
    total = znet[0] + znet[1] + znet[2] + znet[3]
    nsend[...] = total

    def n_copy(to, slot):
        return pltpu.make_async_remote_copy(
            nsend, nnet.at[slot], few_s.at[3], few_r.at[3], device_id={"dp": to}, device_id_type=MESH
        )

    everyone(lambda d: n_copy(d, me).start())
    nnet[me] = total

    loads[6].wait()
    loads[7].wait()
    for s in range(CAP):
        g = gfull[s]
        ls[s] = stat_decay * ls[s] + (1.0 - stat_decay) * dot(g, g, ((1,), (1,)))
        rs[s] = stat_decay * rs[s] + (1.0 - stat_decay) * dot(g, g, ((0,), (0,)))
    stores += [
        pltpu.make_async_copy(ls, ln_out, out_sem.at[2]),
        pltpu.make_async_copy(rs, rn_out, out_sem.at[3]),
    ]
    stores[2].start()
    stores[3].start()

    arrived(prec, few_r.at[1])
    arrived(nnet.at[pl.ds(0, N - 1)], few_r.at[3])
    norms = jnp.sum(nnet[...], axis=0)

    def pick(i):
        return jnp.sum(jnp.where(lane == i, norms, 0.0), axis=1, keepdims=True)

    scale_q = learn_rate * (jnp.sqrt(pick(0)) / (jnp.sqrt(pick(2)) + graft_eps))
    scale_o = learn_rate * (jnp.sqrt(pick(1)) / (jnp.sqrt(pick(3)) + graft_eps))

    loads[4].wait()
    loads[5].wait()
    class Gather:
        pass

    GQ, GO = Gather(), Gather()
    for g, a, src, dst in ((GQ, Q, wq, wq_out), (GO, O, wo, wo_out)):
        g.a, g.src, g.dst, g.i = a, src, dst, a.sems

    def place_of(g, p, q, r=slice(None), c=None):
        f, s = turn(g.a.f, p), turn(g.a.s, q)
        y, x = (s, f) if g.a.query else (f, s)
        return g.dst.at[r, y * SIDE + x, core if c is None else c]

    def move(g, n, p, q, to, r=slice(None), fresh=False):
        src = g.src.at[r] if fresh else place_of(g, p, q, r)
        return remote(src, place_of(g, p, q, r), w_s.at[g.i], w_r.at[g.i, n], to)

    def incoming(g, n, p, q):
        arrived(place_of(g, p, q), w_r.at[g.i, n])

    def share(g, p, q, fresh=False):
        src = g.src if fresh else place_of(g, p, q)
        launch(remote(src, place_of(g, p, q), x_s.at[g.i], x_r.at[g.i], partner))

    gathers = (GQ, GO)

    def spread(g, p, fresh=False):
        base = 3 + 3 * (p % SIDE)
        launch(move(g, base + 0, p, 0, g.a.up, fresh=fresh))
        launch(move(g, base + 1, p, 0, g.a.down, fresh=fresh))

    def relay(g, p):
        base = 3 + 3 * (p % SIDE)
        lo, hi = halves(g.src)
        incoming(g, base + 0, p, -1)
        launch(move(g, base + 2, p, -1, g.a.up, lo))
        incoming(g, base + 1, p, 1)
        launch(move(g, base + 2, p, 1, g.a.down, hi))
        share(g, p, -1)
        share(g, p, 1)

    def far(g, p):
        incoming(g, 5 + 3 * (p % SIDE), p, 2)
        share(g, p, 2)

    def masters_query():
        for r in range(8):
            for c in range(2):
                cols = slice(c * BLK, (c + 1) * BLK)
                fresh = qm[r, :, cols] - scale_q * prec[key[0, r * 2 + c]]
                qm[r, :, cols] = fresh
                wq[r, :, cols] = fresh.astype(jnp.bfloat16)

    def masters_output():
        for r in range(2):
            for c in range(8):
                cols = slice(c * BLK, (c + 1) * BLK)
                fresh = om[r, :, cols] - scale_o * prec[key[0, QB + r * 8 + c]]
                om[r, :, cols] = fresh
                wo[r, :, cols] = fresh.astype(jnp.bfloat16)

    for g, masters in ((GQ, masters_query), (GO, masters_output)):
        masters()
        launch(move(g, 0, 0, 0, g.a.plus, fresh=True))
        launch(move(g, 1, 0, 0, g.a.minus, fresh=True))
        spread(g, 0, fresh=True)
        share(g, 0, 0, fresh=True)
    stores += [
        pltpu.make_async_copy(qm, mq_out, out_sem.at[4]),
        pltpu.make_async_copy(om, mo_out, out_sem.at[5]),
        pltpu.make_async_copy(wq, place_of(GQ, 0, 0), out_sem.at[6]),
        pltpu.make_async_copy(wo, place_of(GO, 0, 0), out_sem.at[7]),
    ]
    for copy in stores[4:]:
        copy.start()
    for g in gathers:
        lo, hi = halves(g.src)
        incoming(g, 0, -1, 0)
        launch(move(g, 2, -1, 0, g.a.plus, lo))
        incoming(g, 1, 1, 0)
        launch(move(g, 2, 1, 0, g.a.minus, hi))
    for g in gathers:
        spread(g, -1)
        spread(g, 1)
        share(g, -1, 0)
        share(g, 1, 0)
    for g in gathers:
        relay(g, 0)
    for g in gathers:
        incoming(g, 2, 2, 0)
        spread(g, 2)
        share(g, 2, 0)
    for p in (-1, 1, 2):
        for g in gathers:
            relay(g, p)
    for p in (0, -1, 1, 2):
        for g in gathers:
            far(g, p)
    for g in gathers:
        arrived(g.dst.at[:, :, other], x_r.at[g.i])
    for a in both:
        left(a.other, pair_s.at[a.sems])
        left(a.s1.at[pl.ds(1, SIDE - 1)], one_s.at[a.sems])
        left(a.t.at[pl.ds(1, SIDE - 1)], two_s.at[a.sems])
    left(gsend.at[pl.ds(0, N - 1)], few_s.at[0])
    left(prec.at[pl.ds(0, (N - 1) * CAP)], few_s.at[1])
    left(znet.at[pl.ds(0, GROUPS - 1)], few_s.at[2])
    left(nnet.at[pl.ds(0, N - 1)], few_s.at[3])
    for g in gathers:
        left(g.dst.at[:, pl.ds(0, 15), core], w_s.at[g.i])
        left(g.dst.at[:, :, core], x_s.at[g.i])
    for copy in stores:
        copy.wait()


def emit(*refs):
    count = (len(refs) - 1) // 2
    sem = refs[-1]
    copies = [pltpu.make_async_copy(refs[i], refs[count + i], sem.at[i]) for i in range(count)]
    for copy in copies:
        copy.start()
    for copy in copies:
        copy.wait()


def on_device(
    grad_query, grad_output, query_master, output_master, query_moment, output_moment,
    left_stat, right_stat, left_root, right_root, owner,
):
    f32, bf16 = jnp.float32, jnp.bfloat16
    stat = (CAP, BLK, BLK)
    qpiece, opiece = query_master.shape, output_master.shape
    anywhere = pl.BlockSpec(memory_space=pl.ANY)
    dma = pltpu.SemaphoreType.DMA

    def sum_scratch(r, w):
        vm = pltpu.VMEM
        chunk, piece = (r, SIDE, HEIGHT, w), (r, HEIGHT, w)
        half = (r // 2, SIDE, HEIGHT, w), (r // 2, HEIGHT, w)
        return (
            vm((SIDE,) + chunk, bf16), vm((SIDE,) + chunk, bf16), vm((SIDE,) + chunk, f32),
            vm((2,) + half[0], f32), vm((2,) + chunk, f32), vm((SIDE,) + piece, f32),
            vm((2,) + half[1], f32), vm((2,) + piece, f32), vm(piece, f32),
        )

    outs = pl.pallas_call(
        kernel,
        out_shape=[
            jax.ShapeDtypeStruct(qpiece, f32),
            jax.ShapeDtypeStruct(opiece, f32),
            jax.ShapeDtypeStruct(qpiece, f32),
            jax.ShapeDtypeStruct(opiece, f32),
            jax.ShapeDtypeStruct((8, 16, 2, HEIGHT, 512), bf16),
            jax.ShapeDtypeStruct((2, 16, 2, HEIGHT, 2048), bf16),
            jax.ShapeDtypeStruct(stat, f32),
            jax.ShapeDtypeStruct(stat, f32),
        ],
        in_specs=[pl.BlockSpec(memory_space=pltpu.HBM)] * 11,
        out_specs=[anywhere] * 8,
        scratch_shapes=[
            *sum_scratch(8, 512),
            *sum_scratch(2, 2048),
            pltpu.VMEM((NB + 1, HEIGHT, BLK), f32),
            pltpu.VMEM((N, CAP, HEIGHT, BLK), f32),
            pltpu.VMEM(stat, f32),
            pltpu.VMEM(stat, f32),
            pltpu.VMEM((N * CAP, HEIGHT, BLK), f32),
            pltpu.VMEM(qpiece, f32),
            pltpu.VMEM(opiece, f32),
            pltpu.VMEM(qpiece, f32),
            pltpu.VMEM(opiece, f32),
            pltpu.VMEM(stat, f32),
            pltpu.VMEM(stat, f32),
            pltpu.VMEM(stat, f32),
            pltpu.VMEM(stat, f32),
            pltpu.VMEM(qpiece, bf16),
            pltpu.VMEM(opiece, bf16),
            pltpu.VMEM((1, 128), f32),
            pltpu.VMEM((GROUPS, 1, 128), f32),
            pltpu.VMEM((1, 128), f32),
            pltpu.VMEM((N, 1, 128), f32),
            pltpu.VMEM((1, NB), jnp.int32),
            pltpu.SMEM((1, NB), jnp.int32),
            pltpu.VMEM((2, 128), jnp.int32),
            pltpu.SMEM((1, 128), jnp.int32),
            pltpu.SMEM((1, 128), jnp.int32),
            dma((8,)),
            dma((8,)),
            dma((4,)),
            dma((2, SIDE)),
            dma((2, SIDE)),
            dma((2,)),
            dma((2, SIDE)),
            dma((2,)),
            dma((2, SIDE, 2)),
            dma((2,)),
            dma((2, 2)),
            dma((4,)),
            dma((4,)),
            dma((2,)),
            dma((2, 15)),
            dma((2,)),
            dma((2,)),
        ],
        compiler_params=pltpu.CompilerParams(collective_id=0, has_side_effects=True, vmem_limit_bytes=LIMIT << 20),
        name="shampoo",
    )(
        *(
            pltpu.with_memory_space_constraint(x, pltpu.HBM)
            for x in (
                owner, grad_query.reshape(1, 8, SIDE, SIDE, 2, HEIGHT, 512),
                grad_output.reshape(1, 2, SIDE, SIDE, 2, HEIGHT, 2048),
                query_master, output_master, query_moment, output_moment,
                left_stat[0, 0], right_stat[0, 0], left_root[0, 0], right_root[0, 0],
            )
        ),
    )
    mq, mo, vq, vo, wq, wo, ln, rn = pl.pallas_call(
        emit,
        out_shape=[jax.ShapeDtypeStruct(x.shape, x.dtype) for x in outs],
        in_specs=[anywhere] * 8,
        out_specs=[pl.BlockSpec(memory_space=pltpu.HBM)] * 8,
        scratch_shapes=[dma((8,))],
        compiler_params=pltpu.CompilerParams(vmem_limit_bytes=1 << 20),
        name="emit",
    )(*outs)
    return mq, mo, vq, vo, wq.reshape(-1, 512), wo.reshape(-1, 2048), ln[None, None], rn[None, None]


def solution(mesh):
    return jax.shard_map(
        on_device,
        mesh=mesh,
        in_specs=(
            P("dp", None, None, "tensor"),
            P("dp", "tensor", None, None),
            P(None, "dp", "tensor"),
            P("tensor", "dp", None),
            P(None, "dp", "tensor"),
            P("tensor", "dp", None),
            P("tensor", "dp", None, None, None),
            P("tensor", "dp", None, None, None),
            P("tensor", "dp", None, None, None),
            P("tensor", "dp", None, None, None),
            P("tensor", None),
        ),
        out_specs=(
            P(None, "dp", "tensor"),
            P("tensor", "dp", None),
            P(None, "dp", "tensor"),
            P("tensor", "dp", None),
            P(None, "tensor"),
            P("tensor", None),
            P("tensor", "dp", None, None, None),
            P("tensor", "dp", None, None, None),
        ),
        check_vma=False,
    )
```
